32 devices in a mesh: dp: 4 (over z), expert: 8 (over y, x, core).
Axes of the slice: x: 2, y: 2, z: 4, core: 2. Of those that a mesh axis runs over, the one named last changes fastest.
Arguments:
- layer_in: bfloat16 [12288, 1536], P(('dp', 'expert')), may hold values from -6 to 6
- grad_out: bfloat16 [12288, 1536], P(('dp', 'expert')), may hold values from -6 to 6
- attn_gain: bfloat16 [1536], P('dp'), may hold values from 0.5 to 1.5
- query_proj: bfloat16 [1536, 1536], P('dp'), may hold values from -0.625 to 0.625
- key_proj: bfloat16 [1536, 512], P('dp'), may hold values from -0.625 to 0.625
- value_proj: bfloat16 [1536, 512], P('dp'), may hold values from -0.15625 to 0.15625
- out_proj: bfloat16 [1536, 1536], P('dp'), may hold values from -2 to 2
- ffn_gain: bfloat16 [1536], P('dp'), may hold values from 0.5 to 1.5
- router_proj: bfloat16 [1536, 16], P('dp'), may hold values from -0.3125 to 0.3125
- gate_up: bfloat16 [16, 1536, 1024], P('expert'), may hold values from -0.15625 to 0.15625
- down_proj: bfloat16 [16, 512, 1536], P('expert'), may hold values from -3 to 3
- routes: int32 [12288, 8], P(('dp', 'expert')), may hold values from 0 to 15, all different within a row
- drop_rank: int32 [32, 3072], P(('dp', 'expert')), may hold values from 0 to 3071, each once within a row
Outputs:
- layer_out: bfloat16 [12288, 1536], P(('dp', 'expert'))
- input_grad: bfloat16 [12288, 1536], P(('dp', 'expert'))
- attngain_grad: float32 [1536], P('dp')
- query_grad: float32 [1536, 1536], P('dp')
- key_grad: float32 [1536, 512], P('dp')
- value_grad: float32 [1536, 512], P('dp')
- outproj_grad: float32 [1536, 1536], P('dp')
- ffngain_grad: float32 [1536], P('dp')
- router_grad: float32 [1536, 16], P('dp')
- gateup_grad: float32 [16, 1536, 1024], P('expert')
- down_grad: float32 [16, 512, 1536], P('expert')
The draws below stay inside these ranges and needn't reach their ends.
Inputs may be any that keep to these rules, and one draw needn't show every extreme that they name: `routes`: each row names 8 different experts. `drop_rank`: each row is a permutation of the 3072 pairs of one block.
All inputs are finite; a program needn't handle non-finite values.
Results may differ from the reference program's by a relative error of at most 0.025.
Values may be sent and summed in bfloat16 or wider, within the bound.
A program may use at most 320 MiB of HBM per device.

```python
import jax
import jax.numpy as jnp
from jax import lax

D = 1536
HEADS = 24
KV_HEADS = 8
HEAD = 64
FF = 512
TOP = 8
PROMPT_DEV = 128
CONT = 512
EXPERTS = 16
TOK_DEV = 384
PROMPT = 1024
BLOCKS = 32
TOKENS = 12288
CAP = 240
N_EXPERT = 8


def shard_levels(own_key, shape, shards, least, top_value):
    gain, own = 1.0, jax.random.fold_in(own_key, 6)
    for dim, parts in shards:
        heights = jnp.exp(jax.random.uniform(jax.random.fold_in(own, dim), (parts,), jnp.float32, least / len(shards), top_value / len(shards)))
        gain = gain * jnp.repeat(heights, shape[dim] // parts).reshape([-1 if axis == dim else 1 for axis in range(len(shape))])
    return gain


def choose_distinct(key, rows, number_of, top, lift):
    sequence = jax.random.permutation(jax.random.fold_in(key, 1), number_of)
    favour = sequence
    for power in range(3):
        favour = favour * favour // number_of
    favour = favour * lift // number_of
    chance = jax.random.randint(jax.random.fold_in(key, 2), (rows, number_of), 0, 4096) + favour
    holders = jax.random.permutation(jax.random.fold_in(key, 3), rows)[jnp.arange(number_of) % rows]
    chance = jnp.where(jnp.arange(rows)[:, None] == holders[None, :], 1 << 14, chance)
    score = chance * number_of + jnp.arange(number_of)
    return lax.top_k(score.astype(jnp.int32), top)[1].astype(jnp.int32)


def scatter_about(stream_key, shape, width, bound, split=(), kind=jnp.bfloat16):
    values = width * jax.random.normal(stream_key, shape, jnp.float32)
    if split:
        values = values * shard_levels(stream_key, shape, split, -0.22, 0.18)
    return jnp.clip(values, -bound, bound).astype(kind)


def setup_inputs(seed: int = 0) -> dict:
    key_of = jax.random.split(jax.random.key(seed), 14)
    return {
        "layer_in": scatter_about(key_of[0], (TOKENS, D), 1.0, 6.0, ((0, 32),)),
        "grad_out": scatter_about(key_of[1], (TOKENS, D), 1.0, 6.0, ((0, 32),)),
        "attn_gain": jnp.clip(1.0 + 0.1 * jax.random.normal(key_of[2], (D,), jnp.float32), 0.5, 1.5).astype(jnp.bfloat16),
        "query_proj": scatter_about(key_of[3], (D, HEADS * HEAD), (D // 16) ** -0.5, 0.625, ((0, 4),)),
        "key_proj": scatter_about(key_of[4], (D, KV_HEADS * HEAD), (D // 16) ** -0.5, 0.625, ((0, 4),)),
        "value_proj": scatter_about(key_of[5], (D, KV_HEADS * HEAD), D ** -0.5, 0.15625, ((0, 4),)),
        "out_proj": scatter_about(key_of[6], (HEADS * HEAD, D), (max(HEADS * HEAD // 192, 1)) ** -0.5, 2.0, ((0, 4),)),
        "ffn_gain": jnp.clip(1.0 + 0.1 * jax.random.normal(key_of[7], (D,), jnp.float32), 0.5, 1.5).astype(jnp.bfloat16),
        "router_proj": scatter_about(key_of[8], (D, EXPERTS), (D // 4) ** -0.5, 0.3125, ((0, 4),)),
        "gate_up": scatter_about(key_of[9], (EXPERTS, D, 2 * FF), D ** -0.5, 0.15625, ((0, 8),)),
        "down_proj": scatter_about(key_of[10], (EXPERTS, FF, D), (max(FF // 128, 1)) ** -0.5, 3.0, ((0, 8),)),
        "routes": choose_distinct(key_of[11], TOKENS, EXPERTS, TOP, 8192),
        "drop_rank": jax.vmap(lambda own: jax.random.permutation(own, TOK_DEV * TOP))(jax.random.split(key_of[12], BLOCKS)).reshape((BLOCKS, TOK_DEV * TOP)).astype(jnp.int32),
    }


@jax.custom_vjp
def low(v):
    return lax.optimization_barrier(v.astype(jnp.bfloat16)).astype(jnp.float32)

@jax.custom_vjp
def low_back(v):
    return v

def low_keep(v):
    return (low(v), None)

def low_pass(kept, grad):
    return (grad,)

def back_keep(v):
    return (v, None)

def back_low(kept, grad):
    return (low(grad),)
low.defvjp(low_keep, low_pass)
low_back.defvjp(back_keep, back_low)
EPSILON = 1e-06
ATTN_SCALE = 0.015625
RESIDUAL = 0.22
ROPE_BASE = 10000.0
MASKED = -1e+30
HIGHEST = lax.Precision.HIGHEST

def product(left, right):
    return jnp.dot(left, right, precision=HIGHEST)

def rms_norm(values, gain_vec):
    inverse = lax.rsqrt(lax.optimization_barrier(jnp.mean(values * values, axis=-1, keepdims=True)) + EPSILON)
    return values * inverse * gain_vec

def token_layout(count):
    token_index = jnp.arange(count, dtype=jnp.int32)
    owner_slot = token_index // TOK_DEV % N_EXPERT
    inner_row = token_index % TOK_DEV
    in_prompt = inner_row < PROMPT_DEV
    half_rows = CONT // 2
    position = jnp.where(in_prompt, owner_slot * PROMPT_DEV + inner_row, PROMPT + owner_slot % 2 * half_rows + inner_row - PROMPT_DEV)
    segment = jnp.where(in_prompt, 0, 1 + owner_slot // 2)
    return (position.astype(jnp.int32), segment.astype(jnp.int32))

def rotate(values, position):
    half_size = HEAD // 2
    frequency = ROPE_BASE ** (-jnp.arange(half_size, dtype=jnp.float32) * 2.0 / HEAD)
    angles = position.astype(jnp.float32)[:, None] * frequency[None, :]
    cosine = jnp.cos(angles)[:, None, :]
    sine_part = jnp.sin(angles)[:, None, :]
    lower_half = values[..., :half_size]
    upper_half = values[..., half_size:]
    return jnp.concatenate([lower_half * cosine - upper_half * sine_part, upper_half * cosine + lower_half * sine_part], axis=-1)

def expert_slots(route_rows, rank_rows, experts, capacity):
    tok_rows, top_count = route_rows.shape
    pair_count = tok_rows * top_count
    expert_flat = route_rows.reshape(pair_count).astype(jnp.int32)
    rank_flat = rank_rows.reshape(pair_count).astype(jnp.int32)
    by_rank = jnp.zeros((pair_count,), jnp.int32).at[rank_flat].set(jnp.arange(pair_count, dtype=jnp.int32))
    ranked_expert = expert_flat[by_rank]
    onehot = (ranked_expert[:, None] == jnp.arange(experts, dtype=jnp.int32)[None, :]).astype(jnp.int32)
    earlier = jnp.cumsum(onehot, axis=0) - onehot
    ranked_slot = lax.optimization_barrier(jnp.sum(earlier * onehot, axis=1)).astype(jnp.int32)
    slot_rank = ranked_slot[rank_flat]
    kept_flag = slot_rank < capacity
    target = jnp.where(kept_flag, expert_flat * capacity + slot_rank, experts * capacity).astype(jnp.int32)
    source_row = jnp.arange(pair_count, dtype=jnp.int32) // top_count
    source = jnp.zeros((experts * capacity + 1,), jnp.int32).at[target].set(source_row)[:experts * capacity]
    filled = jnp.zeros((experts * capacity + 1,), jnp.float32).at[target].set(1.0)[:experts * capacity]
    picked = jnp.minimum(target, experts * capacity - 1).reshape(tok_rows, top_count)
    kept_mask = kept_flag.reshape(tok_rows, top_count).astype(jnp.float32)
    return (source, filled, picked, kept_mask)

def query_block(key_group, value_group, group_position, group_segment, query_rows, query_position, query_segment):
    scores = low_back(ATTN_SCALE * jnp.einsum('tkgd,skd->kgts', query_rows, key_group, precision=HIGHEST))
    allowed = (group_position[None, :] <= query_position[:, None]) & ((group_segment[None, :] == 0) | (group_segment[None, :] == query_segment[:, None]))
    scores = jnp.where(allowed[None, None], scores, MASKED)
    weights = low(jax.nn.softmax(scores, axis=-1))
    return jnp.einsum('kgts,skd->tkgd', weights, value_group, precision=HIGHEST)

def attend_group(query_group, key_group, value_group, group_position, group_segment):
    count = query_group.shape[0]
    blocks = count // TOK_DEV
    checked = jax.checkpoint(query_block)

    def one_block(block_in):
        return checked(key_group, value_group, group_position, group_segment, block_in[0], block_in[1], block_in[2])
    result = lax.map(one_block, (query_group.reshape(blocks, TOK_DEV, KV_HEADS, HEADS // KV_HEADS, HEAD), group_position.reshape(blocks, TOK_DEV), group_segment.reshape(blocks, TOK_DEV)))
    return result.reshape(count, KV_HEADS, HEADS // KV_HEADS, HEAD)

def moe_block(router_proj, gate_up, down_proj, ffn_rows, route_rows, source, filled, picked, kept_mask):
    logits = low_back(product(ffn_rows, router_proj))
    chosen = jnp.take_along_axis(logits, route_rows, axis=1)
    gate_weight = jax.nn.softmax(chosen, axis=-1)
    buffer_rows = low_back(jnp.take(ffn_rows, source, axis=0) * filled[:, None])
    buffer_rows = buffer_rows.reshape(EXPERTS, CAP, D)
    mixed_in = low_back(jnp.einsum('ecd,edf->ecf', buffer_rows, gate_up, precision=HIGHEST))
    acted = low(jax.nn.silu(mixed_in[..., :FF]) * mixed_in[..., FF:])
    produced = low(low_back(jnp.einsum('ecf,efd->ecd', acted, down_proj, precision=HIGHEST)))
    taken = jnp.take(produced.reshape(EXPERTS * CAP, D), picked.reshape(-1), axis=0).reshape(TOK_DEV, TOP, D)
    return lax.optimization_barrier(jnp.sum((gate_weight * kept_mask)[:, :, None] * taken, axis=1))

def forward(layer_in, attn_gain, query_proj, key_proj, value_proj, out_proj, ffn_gain, router_proj, gate_up, down_proj, routes, source, filled, picked, kept_mask):
    normed = low(rms_norm(layer_in, attn_gain))
    queries = low_back(product(normed, query_proj))
    key_raw = low_back(product(normed, key_proj))
    value_all = low(low_back(product(normed, value_proj)))
    position, segment = token_layout(TOKENS)
    query_rot = low(rotate(queries.reshape(TOKENS, HEADS, HEAD), position))
    key_rot = low(rotate(key_raw.reshape(TOKENS, KV_HEADS, HEAD), position))
    group_tokens = TOK_DEV * N_EXPERT
    group_count = TOKENS // group_tokens
    group_position, group_segment = token_layout(group_tokens)

    def one_group(group_in):
        return attend_group(group_in[0], group_in[1], group_in[2], group_position, group_segment)
    attended = lax.map(one_group, (query_rot.reshape(group_count, group_tokens, KV_HEADS, HEADS // KV_HEADS, HEAD), key_rot.reshape(group_count, group_tokens, KV_HEADS, HEAD), value_all.reshape(group_count, group_tokens, KV_HEADS, HEAD)))
    att_low = low(low_back(attended.reshape(TOKENS, HEADS * HEAD)))
    mixed_rows = layer_in + RESIDUAL * low_back(product(att_low, out_proj))
    ffn_in = low(rms_norm(mixed_rows, ffn_gain))
    blocks = TOKENS // TOK_DEV
    checked = jax.checkpoint(moe_block)

    def one_moe(block_in):
        return checked(router_proj, gate_up, down_proj, block_in[0], block_in[1], block_in[2], block_in[3], block_in[4], block_in[5])
    moe_rows = lax.map(one_moe, (ffn_in.reshape(blocks, TOK_DEV, D), routes.reshape(blocks, TOK_DEV, TOP), source, filled, picked, kept_mask))
    return mixed_rows + RESIDUAL * moe_rows.reshape(TOKENS, D)

def reference(layer_in, grad_out, attn_gain, query_proj, key_proj, value_proj, out_proj, ffn_gain, router_proj, gate_up, down_proj, routes, drop_rank):
    blocks = TOKENS // TOK_DEV

    def slot_maker(route_rows, rank_rows):
        return expert_slots(route_rows, rank_rows.reshape(TOK_DEV, TOP), EXPERTS, CAP)
    source, filled, picked, kept_mask = jax.vmap(slot_maker)(routes.reshape(blocks, TOK_DEV, TOP), drop_rank)
    params = tuple((array_in.astype(jnp.float32) for array_in in (layer_in, attn_gain, query_proj, key_proj, value_proj, out_proj, ffn_gain, router_proj, gate_up, down_proj)))

    def run_layer(*values):
        return forward(*values, routes, source, filled, picked, kept_mask)
    layer_out, pullback = jax.vjp(run_layer, *params)
    gradients = pullback(grad_out.astype(jnp.float32))
    return (layer_out.astype(jnp.bfloat16), gradients[0].astype(jnp.bfloat16), gradients[1], gradients[2], gradients[3], gradients[4], gradients[5], gradients[6], gradients[7], gradients[8], gradients[9])
```

```python
import functools

import jax
import jax.numpy as jnp
from jax import lax
from jax.experimental import pallas as pl
from jax.experimental.pallas import tpu as pltpu
from jax.sharding import PartitionSpec as P

HEADS = 24
KV_HEADS = 8
HEAD = 64
PROMPT_DEV = 128


EPSILON = 1e-06
ATTN_SCALE = 0.015625
RESIDUAL = 0.22
ROPE_BASE = 10000.0
MASKED = -1e30
LOG2E = 1.4426950408889634


def norm_forward(inputs, gain_vec):
    inverse = lax.rsqrt(jnp.mean(inputs * inputs, axis=-1, keepdims=True) + EPSILON)
    return (inputs * inverse * gain_vec, inverse)


def norm_backward(inputs, inverse, gain_vec, upstream):
    scaled = upstream * gain_vec
    middle = jnp.mean(inputs * scaled, axis=-1, keepdims=True)
    row_grad = inverse * scaled - inputs * inverse * inverse * inverse * middle
    return (row_grad, jnp.sum(upstream * inputs * inverse, axis=0))


def rotary_tables(position, head_size):
    half_size = head_size // 2
    frequency = ROPE_BASE ** (-jnp.arange(half_size, dtype=jnp.float32) * 2.0 / head_size)
    angles = position.astype(jnp.float32)[:, None] * frequency[None, :]
    return (jnp.cos(angles)[:, None, :], jnp.sin(angles)[:, None, :])


def unrotate(values, cosine, sine_part):
    half_size = values.shape[-1] // 2
    lower_half = values[..., :half_size]
    upper_half = values[..., half_size:]
    return jnp.concatenate(
        [
            lower_half * cosine + upper_half * sine_part,
            upper_half * cosine - lower_half * sine_part,
        ],
        axis=-1,
    )


def slot_codes(routes, ranks, experts, capacity):
    ids = jnp.arange(experts, dtype=jnp.int32)
    hit = routes[:, :, None] == ids[None, None, :]
    far = jnp.int32(routes.shape[0] * routes.shape[1])
    pair_rank = jnp.min(jnp.where(hit, ranks[:, :, None], far), axis=1)
    by_expert = pair_rank.T
    slot = jnp.sum((by_expert[:, :, None] < by_expert[:, None, :]).astype(jnp.int32), axis=1).T
    chosen = pair_rank < far
    return jnp.where(chosen, jnp.where(slot < capacity, 2.0, 1.0), 0.0)


def gates_of(logits, codes):
    chosen = codes > 0.5
    top = jnp.max(jnp.where(chosen, logits, MASKED), axis=-1, keepdims=True)
    raised = jnp.where(chosen, jnp.exp(jnp.minimum(logits - top, 0.0)), 0.0)
    return raised / jnp.sum(raised, axis=-1, keepdims=True)


NT = (((1,), (1,)), ((), ()))
VMEM_GRANT = 50 * 1024 * 1024


def matmul(left, right):
    return jnp.dot(left, right, preferred_element_type=jnp.float32)


def matmul_nt(left, right):
    return lax.dot_general(left, right, NT, preferred_element_type=jnp.float32)


def low_lanes(shape):
    return lax.broadcasted_iota(jnp.int32, shape, 1) % 128 < 64


def spread_pair(pair):
    swapped = pltpu.roll(pair, 64, 1)
    low = low_lanes(pair.shape)
    return jnp.where(low, pair, swapped), jnp.where(low, swapped, pair)


def fold_halves(both, low_out):
    total = both + pltpu.roll(both, 64, 1)
    low = low_lanes(both.shape)
    return jnp.where(low, total, 0.0) if low_out else jnp.where(low, 0.0, total)


def one_half(block, low_half):
    low = low_lanes(block.shape)
    wide = block.astype(jnp.float32)
    wide = jnp.where(low, wide, 0.0) if low_half else jnp.where(low, 0.0, wide)
    return wide.astype(jnp.bfloat16)


def stage_pairs(prompt_ref, tail_ref, spread_ref):
    prompt_total = prompt_ref.shape[0]
    tail_total = tail_ref.shape[0]
    first, second = spread_pair(prompt_ref[...].astype(jnp.float32))
    spread_ref[0, :prompt_total, :] = first.astype(jnp.bfloat16)
    spread_ref[1, :prompt_total, :] = second.astype(jnp.bfloat16)
    first, second = spread_pair(tail_ref[...].astype(jnp.float32))
    spread_ref[0, prompt_total : prompt_total + tail_total, :] = first.astype(jnp.bfloat16)
    spread_ref[1, prompt_total : prompt_total + tail_total, :] = second.astype(jnp.bfloat16)


def attend_kernel(place_ref, q_ref, pk_ref, pv_ref, tk_ref, tv_ref, o_ref, lse_ref, keys, values):
    rows = q_ref.shape[0]
    prompt_rows = PROMPT_DEV
    cont = rows - prompt_rows
    prompt_total = pk_ref.shape[0]
    stage_pairs(pk_ref, tk_ref, keys)
    stage_pairs(pv_ref, tv_ref, values)
    first_position = place_ref[0]
    odd = place_ref[1]
    factor = ATTN_SCALE * LOG2E
    key_at = lax.broadcasted_iota(jnp.int32, (prompt_rows, prompt_total), 1)
    row_at = lax.broadcasted_iota(jnp.int32, (prompt_rows, prompt_total), 0)
    prompt_ok = key_at <= row_at + first_position
    tail_at = lax.broadcasted_iota(jnp.int32, (cont, 2 * cont), 1)
    cont_at = lax.broadcasted_iota(jnp.int32, (cont, 2 * cont), 0)
    tail_ok = ((tail_at < cont) & (odd == 1)) | ((tail_at >= cont) & (tail_at - cont <= cont_at))
    lane = lax.broadcasted_iota(jnp.int32, (rows, 128), 1)
    stats = jnp.zeros((rows, 128), jnp.float32)
    for block in range(3):
        q_block = q_ref[:, block * 128 : block * 128 + 128]
        halves = []
        for half in range(2):
            head = 2 * block + half
            own = head // 3
            q_own = one_half(q_block, half == 0)
            score = matmul_nt(q_own[:prompt_rows], keys[own, :prompt_total, :])
            score = jnp.where(prompt_ok, score, MASKED)
            top = jnp.max(score, axis=1, keepdims=True)
            raised = jnp.exp2((score - top) * factor)
            total = jnp.sum(raised, axis=1, keepdims=True)
            first_out = matmul(raised.astype(jnp.bfloat16), values[own, :prompt_total, :]) / total
            first_log = top * factor + jnp.log(total) * LOG2E
            q_cont = q_own[prompt_rows:]
            score = matmul_nt(q_cont, keys[own, :prompt_total, :])
            tail_score = matmul_nt(q_cont, keys[own, prompt_total:, :])
            tail_score = jnp.where(tail_ok, tail_score, MASKED)
            top = jnp.maximum(
                jnp.max(score, axis=1, keepdims=True), jnp.max(tail_score, axis=1, keepdims=True)
            )
            raised = jnp.exp2((score - top) * factor)
            tail_raised = jnp.exp2((tail_score - top) * factor)
            total = jnp.sum(raised, axis=1, keepdims=True) + jnp.sum(
                tail_raised, axis=1, keepdims=True
            )
            second_out = matmul(raised.astype(jnp.bfloat16), values[own, :prompt_total, :])
            second_out += matmul(tail_raised.astype(jnp.bfloat16), values[own, prompt_total:, :])
            second_out = second_out / total
            second_log = top * factor + jnp.log(total) * LOG2E
            halves.append(jnp.concatenate([first_out, second_out], axis=0))
            stats = jnp.where(
                lane == head, jnp.concatenate([first_log, second_log], axis=0), stats
            )
        o_ref[:, block * 128 : block * 128 + 128] = jnp.where(
            low_lanes((rows, 128)), halves[0], halves[1]
        ).astype(jnp.bfloat16)
    lse_ref[0] = stats


def attend(place, projected, prompt_pairs, tail_pairs):
    rows = projected.shape[0]
    width = HEADS * HEAD
    prompt_total = prompt_pairs.shape[0]
    tail_total = tail_pairs.shape[0]
    pairs = KV_HEADS // 2
    per_pair = width // pairs
    key_total = prompt_total + tail_total
    cost = 4 * HEADS * rows * key_total * 64
    return pl.pallas_call(
        attend_kernel,
        grid=(pairs,),
        in_specs=[
            pl.BlockSpec(memory_space=pltpu.SMEM),
            pl.BlockSpec((rows, per_pair), lambda p: (0, p)),
            pl.BlockSpec((prompt_total, 128), lambda p: (0, p)),
            pl.BlockSpec((prompt_total, 128), lambda p: (0, p + pairs)),
            pl.BlockSpec((tail_total, 128), lambda p: (0, p)),
            pl.BlockSpec((tail_total, 128), lambda p: (0, p + pairs)),
        ],
        out_specs=[
            pl.BlockSpec((rows, per_pair), lambda p: (0, p)),
            pl.BlockSpec((1, rows, 128), lambda p: (p, 0, 0)),
        ],
        out_shape=[
            jax.ShapeDtypeStruct((rows, width), jnp.bfloat16),
            jax.ShapeDtypeStruct((pairs, rows, 128), jnp.float32),
        ],
        scratch_shapes=[
            pltpu.VMEM((2, key_total, 128), jnp.bfloat16),
            pltpu.VMEM((2, key_total, 128), jnp.bfloat16),
        ],
        compiler_params=pltpu.CompilerParams(vmem_limit_bytes=VMEM_GRANT),
        cost_estimate=pl.CostEstimate(
            flops=cost, bytes_accessed=6 * rows * width, transcendentals=HEADS * rows * key_total
        ),
        name="attend",
    )(place, projected, prompt_pairs, prompt_pairs, tail_pairs, tail_pairs)


def attend_back_kernel(
    place_ref,
    q_ref,
    do_ref,
    pk_ref,
    pv_ref,
    tk_ref,
    tv_ref,
    lse_ref,
    cos_ref,
    sin_ref,
    dq_ref,
    dpk_ref,
    dpv_ref,
    dtk_ref,
    dtv_ref,
    keys,
    values,
    keys_across,
    key_sums,
    value_sums,
):
    rows = q_ref.shape[0]
    prompt_rows = PROMPT_DEV
    cont = rows - prompt_rows
    prompt_total = pk_ref.shape[0]
    key_total = prompt_total + tk_ref.shape[0]
    stage_pairs(pk_ref, tk_ref, keys)
    stage_pairs(pv_ref, tv_ref, values)
    first_position = place_ref[0]
    odd = place_ref[1]
    factor = ATTN_SCALE * LOG2E
    keys_across[:, :prompt_total] = pk_ref[...].astype(jnp.float32).T.astype(jnp.bfloat16)
    keys_across[:, prompt_total:] = tk_ref[...].astype(jnp.float32).T.astype(jnp.bfloat16)
    key_at = lax.broadcasted_iota(jnp.int32, (prompt_total, prompt_rows), 0)
    row_at = lax.broadcasted_iota(jnp.int32, (prompt_total, prompt_rows), 1)
    prompt_ok = key_at <= row_at + first_position
    tail_at = lax.broadcasted_iota(jnp.int32, (2 * cont, cont), 0)
    cont_at = lax.broadcasted_iota(jnp.int32, (2 * cont, cont), 1)
    tail_ok = ((tail_at < cont) & (odd == 1)) | ((tail_at >= cont) & (tail_at - cont <= cont_at))
    stats = lse_ref[0]
    query_parts = {}
    for own in range(2):
        across = keys_across[64 * own : 64 * own + 64, :]
        for member in range(3):
            head = 3 * own + member
            block, half = head // 2, head % 2
            lanes = slice(block * 128, block * 128 + 128)
            q_own = one_half(q_ref[:, lanes], half == 0)
            do_own = one_half(do_ref[:, lanes], half == 0)
            log_row = stats[head : head + 1, :]
            q_cont, do_cont = q_own[prompt_rows:], do_own[prompt_rows:]
            log_cont = log_row[:, prompt_rows:]
            score = matmul_nt(keys[own], q_cont)
            weight_prompt = jnp.exp2(score[:prompt_total] * factor - log_cont)
            weight_tail = jnp.where(
                tail_ok, jnp.exp2(jnp.minimum(score[prompt_total:] * factor - log_cont, 0.0)), 0.0
            )
            weight = jnp.concatenate([weight_prompt, weight_tail], axis=0)
            change = matmul_nt(values[own], do_cont)
            delta = jnp.sum(weight * change, axis=0, keepdims=True)
            score_grad = (weight * (change - delta)).astype(jnp.bfloat16)
            key_part = matmul(score_grad, q_cont)
            value_part = matmul(weight.astype(jnp.bfloat16), do_cont)
            query_cont = matmul(across, score_grad)
            if member == 0:
                key_sums[own] = key_part
                value_sums[own] = value_part
            else:
                key_sums[own] += key_part
                value_sums[own] += value_part
            q_first, do_first = q_own[:prompt_rows], do_own[:prompt_rows]
            log_first = log_row[:, :prompt_rows]
            score = matmul_nt(keys[own, :prompt_total, :], q_first)
            weight = jnp.where(
                prompt_ok, jnp.exp2(jnp.minimum(score * factor - log_first, 0.0)), 0.0
            )
            change = matmul_nt(values[own, :prompt_total, :], do_first)
            delta = jnp.sum(weight * change, axis=0, keepdims=True)
            score_grad = (weight * (change - delta)).astype(jnp.bfloat16)
            key_sums[own, :prompt_total, :] += matmul(score_grad, q_first)
            value_sums[own, :prompt_total, :] += matmul(weight.astype(jnp.bfloat16), do_first)
            query_first = matmul(across[:, :prompt_total], score_grad)
            query_parts[head] = jnp.concatenate([query_first, query_cont], axis=1)
    for block in range(3):
        lanes = slice(block * 128, block * 128 + 128)
        turned = jnp.concatenate([query_parts[2 * block], query_parts[2 * block + 1]], axis=0)
        flat = turned.T * ATTN_SCALE
        dq_ref[:, lanes] = turn(flat, cos_ref[...], sin_ref[...]).astype(jnp.bfloat16)
    key_pair = fold_halves(key_sums[0], True) + fold_halves(key_sums[1], False)
    key_pair = key_pair * ATTN_SCALE
    value_pair = fold_halves(value_sums[0], True) + fold_halves(value_sums[1], False)
    dpk_ref[...] = key_pair[:prompt_total].astype(jnp.bfloat16)
    dtk_ref[...] = key_pair[prompt_total:]
    dpv_ref[...] = value_pair[:prompt_total].astype(jnp.bfloat16)
    dtv_ref[...] = value_pair[prompt_total:]


def attend_back(place, projected, upstream, prompt_pairs, tail_pairs, stats, cosines, sines):
    rows, width = upstream.shape
    prompt_total = prompt_pairs.shape[0]
    kv_width = KV_HEADS * HEAD
    tail_total = tail_pairs.shape[0]
    pairs = KV_HEADS // 2
    per_pair = width // pairs
    key_total = prompt_total + tail_total
    across = stats[:, :, :8].transpose(0, 2, 1)
    own_rows = pl.BlockSpec((rows, per_pair), lambda p: (0, p))
    prompt_spec = pl.BlockSpec((prompt_total, 128), lambda p: (0, p))
    tail_spec = pl.BlockSpec((tail_total, 128), lambda p: (0, p))
    table = pl.BlockSpec((rows, 128), lambda p: (0, 0))
    return pl.pallas_call(
        attend_back_kernel,
        grid=(pairs,),
        in_specs=[
            pl.BlockSpec(memory_space=pltpu.SMEM),
            own_rows,
            own_rows,
            prompt_spec,
            pl.BlockSpec((prompt_total, 128), lambda p: (0, p + pairs)),
            tail_spec,
            pl.BlockSpec((tail_total, 128), lambda p: (0, p + pairs)),
            pl.BlockSpec((1, 8, rows), lambda p: (p, 0, 0)),
            table,
            table,
        ],
        out_specs=[own_rows, prompt_spec, prompt_spec, tail_spec, tail_spec],
        out_shape=[
            jax.ShapeDtypeStruct((rows, width), jnp.bfloat16),
            jax.ShapeDtypeStruct((prompt_total, kv_width), jnp.bfloat16),
            jax.ShapeDtypeStruct((prompt_total, kv_width), jnp.bfloat16),
            jax.ShapeDtypeStruct((tail_total, kv_width), jnp.float32),
            jax.ShapeDtypeStruct((tail_total, kv_width), jnp.float32),
        ],
        scratch_shapes=[
            pltpu.VMEM((2, key_total, 128), jnp.bfloat16),
            pltpu.VMEM((2, key_total, 128), jnp.bfloat16),
            pltpu.VMEM((128, key_total), jnp.bfloat16),
            pltpu.VMEM((2, key_total, 128), jnp.float32),
            pltpu.VMEM((2, key_total, 128), jnp.float32),
        ],
        compiler_params=pltpu.CompilerParams(vmem_limit_bytes=VMEM_GRANT),
        cost_estimate=pl.CostEstimate(
            flops=10 * HEADS * rows * key_total * 64,
            bytes_accessed=12 * rows * width,
            transcendentals=HEADS * rows * key_total,
        ),
        name="attend_back",
    )(
        place,
        projected,
        upstream,
        prompt_pairs,
        prompt_pairs,
        tail_pairs,
        tail_pairs,
        across,
        cosines,
        sines,
    )


def pair_tables(position):
    frequency = ROPE_BASE ** (-jnp.arange(HEAD // 2, dtype=jnp.float32) * 2.0 / HEAD)
    angles = position.astype(jnp.float32)[:, None] * frequency[None, :]
    cosine, sine = jnp.cos(angles), jnp.sin(angles)
    return (
        jnp.concatenate([cosine, cosine, cosine, cosine], axis=1),
        jnp.concatenate([sine, -sine, sine, -sine], axis=1),
    )


def turn(flat, cosines, sines):
    front = lax.broadcasted_iota(jnp.int32, flat.shape, 1) % 64 < 32
    partner = jnp.where(front, pltpu.roll(flat, 96, 1), pltpu.roll(flat, 32, 1))
    return flat * cosines + partner * sines


def project_kernel(turned_blocks, x_ref, w_ref, cos_ref, sin_ref, o_ref):
    made = matmul(x_ref[...], w_ref[...])
    rotates = pl.program_id(0) < turned_blocks
    for lanes in (slice(0, 128), slice(128, 256)):
        part = made[:, lanes]
        o_ref[:, lanes] = jnp.where(
            rotates, turn(part, cos_ref[...], -sin_ref[...]), part
        ).astype(jnp.bfloat16)


def project(normed, weights, cosines, sines):
    rows, width = normed.shape
    columns = (HEADS + 2 * KV_HEADS) * HEAD
    table = pl.BlockSpec((rows, 128), lambda j: (0, 0))
    return pl.pallas_call(
        functools.partial(project_kernel, (HEADS + KV_HEADS) * HEAD // 256),
        grid=(columns // 256,),
        in_specs=[
            pl.BlockSpec((rows, width), lambda j: (0, 0)),
            pl.BlockSpec((width, 256), lambda j: (0, j)),
            table,
            table,
        ],
        out_specs=pl.BlockSpec((rows, 256), lambda j: (0, j)),
        out_shape=jax.ShapeDtypeStruct((rows, columns), jnp.bfloat16),
        compiler_params=pltpu.CompilerParams(vmem_limit_bytes=VMEM_GRANT),
        cost_estimate=pl.CostEstimate(
            flops=2 * rows * width * columns, bytes_accessed=2 * width * columns, transcendentals=0
        ),
        name="project",
    )(normed, weights, cosines, sines)


def experts_kernel(
    place_ref, x_ref, g_ref, up_ref, down_ref, router_ref, codes_ref, dx_ref, dgu_ref, act_ref
):
    local_experts, hidden = down_ref.shape[0], down_ref.shape[1]
    width = x_ref.shape[1]
    x, g = x_ref[...], g_ref[...]
    logits = matmul(x, router_ref[...])
    codes = codes_ref[...].astype(jnp.float32)
    gates = gates_of(logits, codes)
    kept = codes > 1.5
    lane = lax.broadcasted_iota(jnp.int32, logits.shape, 1)
    placed = jnp.zeros(logits.shape, jnp.float32)
    total = None
    for local in range(local_experts):
        number = place_ref[2] + local
        mine = (lane == number) & kept
        weight = jnp.sum(jnp.where(mine, gates, 0.0), axis=1, keepdims=True)
        made = matmul(x, up_ref[local])
        act_grad = matmul_nt(g, down_ref[local])
        gate_part, up_part = made[:, :hidden], made[:, hidden:]
        sigma = jax.nn.sigmoid(gate_part)
        silu = gate_part * sigma
        acted = (silu * up_part).astype(jnp.bfloat16).astype(jnp.float32)
        act_ref[local] = (weight * acted).astype(jnp.bfloat16)
        pair_grad = RESIDUAL * jnp.sum(acted * act_grad, axis=1, keepdims=True)
        placed = jnp.where(mine, pair_grad, placed)
        scaled = (RESIDUAL * weight) * act_grad
        gate_grad = scaled * up_part * sigma * (1.0 + gate_part * (1.0 - sigma))
        both = jnp.concatenate([gate_grad, scaled * silu], axis=1).astype(jnp.bfloat16)
        dgu_ref[local] = both
        part = matmul_nt(both, up_ref[local])
        total = part if total is None else total + part
    dx_ref[:, :width] = total.astype(jnp.bfloat16)
    high = placed.astype(jnp.bfloat16).astype(jnp.float32)
    rest = pltpu.roll(placed - high, 64, 1)
    dx_ref[:, width:] = (high + rest).astype(jnp.bfloat16)


def experts(place, rows_in, rows_grad, gate_up, down, weights, codes):
    total, width = rows_in.shape
    local_experts, hidden = down.shape[0], down.shape[1]
    step = 256
    whole = pl.Buffered(1)
    return pl.pallas_call(
        experts_kernel,
        grid=(total // step,),
        in_specs=[
            pl.BlockSpec(memory_space=pltpu.SMEM),
            pl.BlockSpec((step, width), lambda i: (i, 0)),
            pl.BlockSpec((step, width), lambda i: (i, 0)),
            pl.BlockSpec(gate_up.shape, lambda i: (0, 0, 0), pipeline_mode=whole),
            pl.BlockSpec(down.shape, lambda i: (0, 0, 0), pipeline_mode=whole),
            pl.BlockSpec((width, 128), lambda i: (0, 0), pipeline_mode=whole),
            pl.BlockSpec((step, 128), lambda i: (i, 0)),
        ],
        out_specs=[
            pl.BlockSpec((step, width + 128), lambda i: (i, 0)),
            pl.BlockSpec((local_experts, step, 2 * hidden), lambda i: (0, i, 0)),
            pl.BlockSpec((local_experts, step, hidden), lambda i: (0, i, 0)),
        ],
        out_shape=[
            jax.ShapeDtypeStruct((total, width + 128), jnp.bfloat16),
            jax.ShapeDtypeStruct((local_experts, total, 2 * hidden), jnp.bfloat16),
            jax.ShapeDtypeStruct((local_experts, total, hidden), jnp.bfloat16),
        ],
        compiler_params=pltpu.CompilerParams(vmem_limit_bytes=VMEM_GRANT),
        cost_estimate=pl.CostEstimate(
            flops=10 * total * width * local_experts * hidden,
            bytes_accessed=16 * total * width,
            transcendentals=total * local_experts * hidden,
        ),
        name="experts",
    )(place, rows_in, rows_grad, gate_up, down, weights, codes)


def dense_grads_kernel(
    normed_ref, ffn_ref, att_ref, right_ref, out_right_ref, extra_ref, o_ref, *, mixed
):
    block = pl.program_id(0)

    @pl.when(block < mixed)
    def _():
        o_ref[...] = matmul(normed_ref[...], right_ref[...]).astype(jnp.bfloat16)

    @pl.when(block == mixed)
    def _():
        o_ref[:, :256] = matmul(normed_ref[...], right_ref[:, :256]).astype(jnp.bfloat16)
        o_ref[:, 256:] = (matmul(ffn_ref[...], right_ref[:, 256:]) + extra_ref[...]).astype(
            jnp.bfloat16
        )

    @pl.when(block > mixed)
    def _():
        o_ref[...] = matmul(att_ref[...], out_right_ref[...]).astype(jnp.bfloat16)


def dense_weight_grads(normed, ffn_in, attended, right, out_right, extra):
    features, rows = normed.shape
    mixed = right.shape[1] // 384 - 1
    columns = right.shape[1] + out_right.shape[1]
    whole = pl.BlockSpec((features, rows), lambda j: (0, 0))
    return pl.pallas_call(
        functools.partial(dense_grads_kernel, mixed=mixed),
        grid=(columns // 384,),
        in_specs=[
            whole,
            whole,
            whole,
            pl.BlockSpec((rows, 384), lambda j: (0, jnp.minimum(j, mixed))),
            pl.BlockSpec((rows, 384), lambda j: (0, jnp.maximum(j - mixed - 1, 0))),
            pl.BlockSpec((features, 128), lambda j: (0, 0)),
        ],
        out_specs=pl.BlockSpec((features, 384), lambda j: (0, j)),
        out_shape=jax.ShapeDtypeStruct((features, columns), jnp.bfloat16),
        compiler_params=pltpu.CompilerParams(vmem_limit_bytes=VMEM_GRANT),
        cost_estimate=pl.CostEstimate(
            flops=2 * features * rows * columns,
            bytes_accessed=2 * features * columns,
            transcendentals=0,
        ),
        name="dense_weight_grads",
    )(normed, ffn_in, attended, right, out_right, extra)


def on_device(
    layer_in,
    grad_out,
    attn_gain,
    query_proj,
    key_proj,
    value_proj,
    out_proj,
    ffn_gain,
    router_proj,
    gate_up,
    down_proj,
    routes,
    drop_rank,
):
    tok_rows, width = layer_in.shape
    local_experts = gate_up.shape[0]
    hidden_units = down_proj.shape[1]
    top_count = routes.shape[1]
    owner_count = lax.axis_size("expert")
    owner_index = lax.axis_index("expert")
    expert_total = local_experts * owner_count
    capacity = 5 * tok_rows * top_count // (4 * expert_total)
    prompt_rows = PROMPT_DEV
    half_rows = tok_rows - prompt_rows
    prompt_total = prompt_rows * owner_count
    head_size = HEAD
    kv_heads = KV_HEADS
    kv_width = kv_heads * head_size
    dp_count = lax.axis_size("dp")
    shard_rows = query_proj.shape[0]
    piece_rows = shard_rows // owner_count

    def whole_of(shard):
        columns = shard.shape[1]
        piece = lax.dynamic_slice_in_dim(shard, owner_index * piece_rows, piece_rows, 0)
        piece = lax.all_gather(piece, "dp", axis=0, tiled=True)
        piece = lax.all_gather(piece, "expert", axis=0, tiled=True)
        piece = piece.reshape(owner_count, dp_count, piece_rows, columns)
        return piece.transpose(1, 0, 2, 3).reshape(dp_count * shard_rows, columns)

    extras = jnp.concatenate(
        [
            router_proj,
            attn_gain[:, None],
            ffn_gain[:, None],
            jnp.zeros((shard_rows, 126 - router_proj.shape[1]), jnp.bfloat16),
        ],
        axis=1,
    )
    fused = whole_of(jnp.concatenate([query_proj, key_proj, value_proj], axis=1))
    spread = lax.dynamic_update_slice(
        jnp.zeros((dp_count * shard_rows, 128), jnp.bfloat16),
        extras,
        (lax.axis_index("dp") * shard_rows, 0),
    )
    extra_full = lax.psum(spread, "dp")
    full_out = whole_of(out_proj)
    codes = slot_codes(routes, drop_rank.reshape(tok_rows, top_count), expert_total, capacity)
    codes_all = lax.all_gather(
        jnp.pad(codes, ((0, 0), (0, 128 - expert_total))).astype(jnp.bfloat16),
        "expert",
        axis=0,
        tiled=True,
    )
    fused, codes_all = lax.optimization_barrier((fused, codes_all))
    q_width = query_proj.shape[1]
    extra_at = q_width + 2 * kv_width
    full_router = extra_full[:, :expert_total]
    gain_one = extra_full[:, expert_total]
    gain_two = extra_full[:, expert_total + 1]
    grad_all = lax.all_gather(grad_out, "expert", axis=0, tiled=True)
    gain_one = gain_one.astype(jnp.float32)
    gain_two = gain_two.astype(jnp.float32)
    inputs = layer_in.astype(jnp.float32)
    normed_full, inverse_one = norm_forward(inputs, gain_one)
    normed = normed_full.astype(jnp.bfloat16)
    row_index = jnp.arange(tok_rows, dtype=jnp.int32)
    parity = owner_index % 2
    position = jnp.where(
        row_index < prompt_rows,
        owner_index * prompt_rows + row_index,
        prompt_total + parity * half_rows + row_index - prompt_rows,
    )
    place = jnp.stack(
        [owner_index * prompt_rows, parity, owner_index * local_experts]
    ).astype(jnp.int32)
    cosines, sines = pair_tables(position)
    projected = project(normed, fused, cosines, sines)
    own_pairs = projected[:, q_width:]
    prompt_pairs = lax.all_gather(own_pairs[:prompt_rows], "expert", axis=0, tiled=True)
    ahead = [(source, source + 1) for source in range(0, owner_count, 2)]
    partner_pairs = lax.ppermute(own_pairs[prompt_rows:], "expert", ahead)
    tail_pairs = jnp.concatenate([partner_pairs, own_pairs[prompt_rows:]], axis=0)
    att_low, stats = attend(place, projected, prompt_pairs, tail_pairs)
    attn_proj = jnp.dot(att_low, full_out, preferred_element_type=jnp.float32)
    mixed_rows = inputs + RESIDUAL * attn_proj
    ffn_full, inverse_two = norm_forward(mixed_rows, gain_two)
    ffn_low = ffn_full.astype(jnp.bfloat16)
    ffn_low, grad_all = lax.optimization_barrier((ffn_low, grad_all))
    ffn_all = lax.all_gather(ffn_low, "expert", axis=0, tiled=True)
    gates = gates_of(
        jnp.dot(ffn_low, full_router, preferred_element_type=jnp.float32), codes
    )
    input_rows, mixed_grad, acted_low = experts(
        place, ffn_all, grad_all, gate_up, down_proj, extra_full, codes_all
    )
    back_rows = lax.psum_scatter(
        input_rows, "expert", scatter_dimension=0, tiled=True
    ).astype(jnp.float32)
    gateup_local = jnp.einsum(
        "td,etf->edf", ffn_all, mixed_grad, preferred_element_type=jnp.float32
    )
    down_local = RESIDUAL * jnp.einsum(
        "etf,td->efd", acted_low, grad_all, preferred_element_type=jnp.float32
    )
    upstream = grad_out.astype(jnp.float32)
    gate_grad = (
        back_rows[:, width : width + expert_total]
        + back_rows[:, width + 64 : width + 64 + expert_total]
    )
    logit_grad = (
        gates * (gate_grad - jnp.sum(gates * gate_grad, axis=1, keepdims=True))
    ).astype(jnp.bfloat16)
    ffn_grad = jnp.einsum("te,de->td", logit_grad, full_router, preferred_element_type=jnp.float32)
    ffn_grad = ffn_grad + back_rows[:, :width]
    norm_part, gain_two_local = norm_backward(mixed_rows, inverse_two, gain_two, ffn_grad)
    mixed_grad_total = upstream + norm_part
    attn_grad_low = (RESIDUAL * mixed_grad_total).astype(jnp.bfloat16)
    moe_part = jnp.einsum(
        "etf,efd->td", acted_low, down_proj, preferred_element_type=jnp.float32
    ).astype(jnp.bfloat16)
    gateup_low = gateup_local.astype(jnp.bfloat16).reshape(-1, 2 * hidden_units)
    down_low = down_local.astype(jnp.bfloat16).reshape(-1, width)
    unit = gateup_low.shape[0] // 192
    down_cut = down_low.shape[0] // 64 * 43
    parts = [
        (gateup_low[: 40 * unit],),
        (gateup_low[40 * unit : 112 * unit],),
        (gateup_low[112 * unit : 183 * unit],),
        (gateup_low[183 * unit :], down_low[:down_cut]),
        (down_low[down_cut:],),
    ]
    attended_grad = jnp.einsum(
        "td,cd->tc", attn_grad_low, full_out, preferred_element_type=jnp.float32
    ).astype(jnp.bfloat16)
    sums = [lax.psum(parts[0], "dp")]
    attended_grad, moe_part, sums, parts = lax.optimization_barrier(
        (attended_grad, moe_part, sums, parts)
    )
    for part in parts[1:]:
        part, sums[-1] = lax.optimization_barrier((part, sums[-1]))
        sums.append(lax.psum(part, "dp"))
    gateup_grad = jnp.concatenate([sums[0][0], sums[1][0], sums[2][0], sums[3][0]], axis=0)
    gateup_grad = gateup_grad.astype(jnp.float32).reshape(gate_up.shape)
    down_grad = jnp.concatenate([sums[3][1], sums[4][0]], axis=0)
    down_grad = down_grad.astype(jnp.float32).reshape(down_proj.shape)

    def by_piece(values):
        turned = values.T.reshape(dp_count, owner_count, piece_rows, tok_rows)
        return turned.transpose(1, 0, 2, 3).reshape(width, tok_rows)

    query_grad_low, prompt_key_part, prompt_value_part, tail_key_part, tail_value_part = (
        attend_back(
            place, projected, attended_grad, prompt_pairs, tail_pairs, stats, cosines, sines
        )
    )
    moe_rows = lax.psum_scatter(moe_part, "expert", scatter_dimension=0, tiled=True)
    moe_rows, prompt_key_part = lax.optimization_barrier((moe_rows, prompt_key_part))
    prompt_grad = lax.psum_scatter(
        jnp.concatenate([prompt_key_part, prompt_value_part], axis=1),
        "expert",
        scatter_dimension=0,
        tiled=True,
    )
    layer_out = (mixed_rows + RESIDUAL * moe_rows.astype(jnp.float32)).astype(jnp.bfloat16)
    prompt_grad = prompt_grad.astype(jnp.float32)
    tail_part = jnp.concatenate([tail_key_part, tail_value_part], axis=1)
    behind = [(source + 1, source) for source in range(0, owner_count, 2)]
    tail_grad = tail_part[half_rows:] + lax.ppermute(
        tail_part[:half_rows].astype(jnp.bfloat16), "expert", behind
    ).astype(jnp.float32)
    pair_grad = jnp.concatenate([prompt_grad, tail_grad], axis=0)
    cosine, sine_part = rotary_tables(position, head_size)
    key_grad_low = (
        unrotate(pair_grad[:, :kv_width].reshape(tok_rows, kv_heads, head_size), cosine, sine_part)
        .reshape(tok_rows, kv_width)
        .astype(jnp.bfloat16)
    )
    value_grad_low = pair_grad[:, kv_width:].astype(jnp.bfloat16)
    all_grad = jnp.concatenate(
        [
            query_grad_low,
            key_grad_low,
            value_grad_low,
            jnp.pad(logit_grad, ((0, 0), (0, 128 - expert_total))),
        ],
        axis=1,
    )
    normed_grad = jnp.einsum(
        "tc,dc->td",
        all_grad[:, :extra_at],
        fused,
        preferred_element_type=jnp.float32,
    )
    input_part, gain_one_local = norm_backward(inputs, inverse_one, gain_one, normed_grad)
    input_grad = (mixed_grad_total + input_part).astype(jnp.bfloat16)

    def summed(pieces):
        pieces = lax.psum_scatter(pieces, "expert", scatter_dimension=0, tiled=True)
        pieces = lax.psum_scatter(pieces, "dp", scatter_dimension=0, tiled=True)
        return lax.all_gather(pieces, "expert", axis=0, tiled=True).astype(jnp.float32)

    extra = jnp.stack([gain_one_local, gain_two_local], axis=1)
    extra = extra.reshape(dp_count, owner_count, piece_rows, 2).transpose(1, 0, 2, 3)
    extra = jnp.pad(
        extra.reshape(width, 2), ((0, 0), (expert_total, 126 - expert_total))
    )
    late = summed(
        dense_weight_grads(
            by_piece(normed), by_piece(ffn_low), by_piece(att_low), all_grad, attn_grad_low, extra
        )
    )
    dense_grads = (
        late[:, extra_at + expert_total],
        late[:, :q_width],
        late[:, q_width : q_width + kv_width],
        late[:, q_width + kv_width : extra_at],
        late[:, extra_at + 128 :],
        late[:, extra_at + expert_total + 1],
        late[:, extra_at : extra_at + expert_total],
    )
    return (
        layer_out,
        input_grad,
        dense_grads[0],
        dense_grads[1],
        dense_grads[2],
        dense_grads[3],
        dense_grads[4],
        dense_grads[5],
        dense_grads[6],
        gateup_grad,
        down_grad,
    )


def solution(mesh):
    placed = (
        P(("dp", "expert"), None),
        P(("dp", "expert"), None),
        P("dp"),
        P("dp", None),
        P("dp", None),
        P("dp", None),
        P("dp", None),
        P("dp"),
        P("dp", None),
        P("expert", None, None),
        P("expert", None, None),
        P(("dp", "expert"), None),
        P(("dp", "expert"), None),
    )
    return jax.shard_map(
        on_device,
        mesh=mesh,
        in_specs=placed,
        out_specs=(
            P(("dp", "expert"), None),
            P(("dp", "expert"), None),
            P("dp"),
            P("dp", None),
            P("dp", None),
            P("dp", None),
            P("dp", None),
            P("dp"),
            P("dp", None),
            P("expert", None, None),
            P("expert", None, None),
        ),
        check_vma=False,
    )
```

```python
import functools

import jax
import jax.numpy as jnp
from jax import lax
from jax.experimental import pallas as pl
from jax.experimental.pallas import tpu as pltpu
from jax.sharding import PartitionSpec as P

HEADS = 24
KV_HEADS = 8
HEAD = 64
PROMPT_DEV = 128


EPSILON = 1e-06
ATTN_SCALE = 0.015625
RESIDUAL = 0.22
ROPE_BASE = 10000.0
MASKED = -1e30
LOG2E = 1.4426950408889634


def norm_forward(inputs, gain_vec):
    inverse = lax.rsqrt(jnp.mean(inputs * inputs, axis=-1, keepdims=True) + EPSILON)
    return (inputs * inverse * gain_vec, inverse)


def norm_backward(inputs, inverse, gain_vec, upstream):
    scaled = upstream * gain_vec
    middle = jnp.mean(inputs * scaled, axis=-1, keepdims=True)
    row_grad = inverse * scaled - inputs * inverse * inverse * inverse * middle
    return (row_grad, jnp.sum(upstream * inputs * inverse, axis=0))


def rotary_tables(position, head_size):
    half_size = head_size // 2
    frequency = ROPE_BASE ** (-jnp.arange(half_size, dtype=jnp.float32) * 2.0 / head_size)
    angles = position.astype(jnp.float32)[:, None] * frequency[None, :]
    return (jnp.cos(angles)[:, None, :], jnp.sin(angles)[:, None, :])


def unrotate(values, cosine, sine_part):
    half_size = values.shape[-1] // 2
    lower_half = values[..., :half_size]
    upper_half = values[..., half_size:]
    return jnp.concatenate(
        [
            lower_half * cosine + upper_half * sine_part,
            upper_half * cosine - lower_half * sine_part,
        ],
        axis=-1,
    )


def slot_codes(routes, ranks, experts, capacity):
    ids = jnp.arange(experts, dtype=jnp.int32)
    hit = routes[:, :, None] == ids[None, None, :]
    far = jnp.int32(routes.shape[0] * routes.shape[1])
    pair_rank = jnp.min(jnp.where(hit, ranks[:, :, None], far), axis=1)
    by_expert = pair_rank.T
    slot = jnp.sum((by_expert[:, :, None] < by_expert[:, None, :]).astype(jnp.int32), axis=1).T
    chosen = pair_rank < far
    return jnp.where(chosen, jnp.where(slot < capacity, 2.0, 1.0), 0.0)


def gates_of(logits, codes):
    chosen = codes > 0.5
    top = jnp.max(jnp.where(chosen, logits, MASKED), axis=-1, keepdims=True)
    raised = jnp.where(chosen, jnp.exp(jnp.minimum(logits - top, 0.0)), 0.0)
    return raised / jnp.sum(raised, axis=-1, keepdims=True)


NT = (((1,), (1,)), ((), ()))
VMEM_GRANT = 56 * 1024 * 1024
MESH_ID = pl.DeviceIdType.MESH


def matmul(left, right):
    return jnp.dot(left, right, preferred_element_type=jnp.float32)


def matmul_nt(left, right):
    return lax.dot_general(left, right, NT, preferred_element_type=jnp.float32)


def low_lanes(shape):
    return lax.broadcasted_iota(jnp.int32, shape, 1) % 128 < 64


def spread_pair(pair):
    swapped = pltpu.roll(pair, 64, 1)
    low = low_lanes(pair.shape)
    return jnp.where(low, pair, swapped), jnp.where(low, swapped, pair)


def fold_halves(both, low_out):
    total = both + pltpu.roll(both, 64, 1)
    low = low_lanes(both.shape)
    return jnp.where(low, total, 0.0) if low_out else jnp.where(low, 0.0, total)


def one_half(block, low_half):
    low = low_lanes(block.shape)
    wide = block.astype(jnp.float32)
    wide = jnp.where(low, wide, 0.0) if low_half else jnp.where(low, 0.0, wide)
    return wide.astype(jnp.bfloat16)


def stage_pairs(prompt_ref, tail_ref, spread_ref):
    prompt_total = prompt_ref.shape[0]
    tail_total = tail_ref.shape[0]
    first, second = spread_pair(prompt_ref[...].astype(jnp.float32))
    spread_ref[0, :prompt_total, :] = first.astype(jnp.bfloat16)
    spread_ref[1, :prompt_total, :] = second.astype(jnp.bfloat16)
    first, second = spread_pair(tail_ref[...].astype(jnp.float32))
    spread_ref[0, prompt_total : prompt_total + tail_total, :] = first.astype(jnp.bfloat16)
    spread_ref[1, prompt_total : prompt_total + tail_total, :] = second.astype(jnp.bfloat16)


def attend_kernel(place_ref, q_ref, pk_ref, pv_ref, tk_ref, tv_ref, o_ref, lse_ref, keys, values):
    rows = q_ref.shape[0]
    prompt_rows = PROMPT_DEV
    cont = rows - prompt_rows
    prompt_total = pk_ref.shape[0]
    stage_pairs(pk_ref, tk_ref, keys)
    stage_pairs(pv_ref, tv_ref, values)
    first_position = place_ref[0]
    odd = place_ref[1]
    factor = ATTN_SCALE * LOG2E
    key_at = lax.broadcasted_iota(jnp.int32, (prompt_rows, prompt_total), 1)
    row_at = lax.broadcasted_iota(jnp.int32, (prompt_rows, prompt_total), 0)
    prompt_ok = key_at <= row_at + first_position
    tail_at = lax.broadcasted_iota(jnp.int32, (cont, 2 * cont), 1)
    cont_at = lax.broadcasted_iota(jnp.int32, (cont, 2 * cont), 0)
    tail_ok = ((tail_at < cont) & (odd == 1)) | ((tail_at >= cont) & (tail_at - cont <= cont_at))
    lane = lax.broadcasted_iota(jnp.int32, (rows, 128), 1)
    stats = jnp.zeros((rows, 128), jnp.float32)
    for block in range(3):
        q_block = q_ref[:, block * 128 : block * 128 + 128]
        halves = []
        for half in range(2):
            head = 2 * block + half
            own = head // 3
            q_own = one_half(q_block, half == 0)
            score = matmul_nt(q_own[:prompt_rows], keys[own, :prompt_total, :])
            score = jnp.where(prompt_ok, score, MASKED)
            top = jnp.max(score, axis=1, keepdims=True)
            raised = jnp.exp2((score - top) * factor)
            total = jnp.sum(raised, axis=1, keepdims=True)
            first_out = matmul(raised.astype(jnp.bfloat16), values[own, :prompt_total, :]) / total
            first_log = top * factor + jnp.log(total) * LOG2E
            q_cont = q_own[prompt_rows:]
            score = matmul_nt(q_cont, keys[own, :prompt_total, :])
            tail_score = matmul_nt(q_cont, keys[own, prompt_total:, :])
            tail_score = jnp.where(tail_ok, tail_score, MASKED)
            top = jnp.maximum(
                jnp.max(score, axis=1, keepdims=True), jnp.max(tail_score, axis=1, keepdims=True)
            )
            raised = jnp.exp2((score - top) * factor)
            tail_raised = jnp.exp2((tail_score - top) * factor)
            total = jnp.sum(raised, axis=1, keepdims=True) + jnp.sum(
                tail_raised, axis=1, keepdims=True
            )
            second_out = matmul(raised.astype(jnp.bfloat16), values[own, :prompt_total, :])
            second_out += matmul(tail_raised.astype(jnp.bfloat16), values[own, prompt_total:, :])
            second_out = second_out / total
            second_log = top * factor + jnp.log(total) * LOG2E
            halves.append(jnp.concatenate([first_out, second_out], axis=0))
            stats = jnp.where(
                lane == head, jnp.concatenate([first_log, second_log], axis=0), stats
            )
        o_ref[:, block * 128 : block * 128 + 128] = jnp.where(
            low_lanes((rows, 128)), halves[0], halves[1]
        ).astype(jnp.bfloat16)
    lse_ref[0] = stats


def attend(place, projected, prompt_pairs, tail_pairs):
    rows = projected.shape[0]
    width = HEADS * HEAD
    prompt_total = prompt_pairs.shape[0]
    tail_total = tail_pairs.shape[0]
    pairs = KV_HEADS // 2
    per_pair = width // pairs
    key_total = prompt_total + tail_total
    cost = 4 * HEADS * rows * key_total * 64
    return pl.pallas_call(
        attend_kernel,
        grid=(pairs,),
        in_specs=[
            pl.BlockSpec(memory_space=pltpu.SMEM),
            pl.BlockSpec((rows, per_pair), lambda p: (0, p)),
            pl.BlockSpec((prompt_total, 128), lambda p: (0, p)),
            pl.BlockSpec((prompt_total, 128), lambda p: (0, p + pairs)),
            pl.BlockSpec((tail_total, 128), lambda p: (0, p)),
            pl.BlockSpec((tail_total, 128), lambda p: (0, p + pairs)),
        ],
        out_specs=[
            pl.BlockSpec((rows, per_pair), lambda p: (0, p)),
            pl.BlockSpec((1, rows, 128), lambda p: (p, 0, 0)),
        ],
        out_shape=[
            jax.ShapeDtypeStruct((rows, width), jnp.bfloat16),
            jax.ShapeDtypeStruct((pairs, rows, 128), jnp.float32),
        ],
        scratch_shapes=[
            pltpu.VMEM((2, key_total, 128), jnp.bfloat16),
            pltpu.VMEM((2, key_total, 128), jnp.bfloat16),
        ],
        compiler_params=pltpu.CompilerParams(vmem_limit_bytes=VMEM_GRANT),
        cost_estimate=pl.CostEstimate(
            flops=cost, bytes_accessed=6 * rows * width, transcendentals=HEADS * rows * key_total
        ),
        name="attend",
    )(place, projected, prompt_pairs, prompt_pairs, tail_pairs, tail_pairs)


def attend_back_kernel(
    place_ref,
    q_ref,
    do_ref,
    pk_ref,
    pv_ref,
    tk_ref,
    tv_ref,
    lse_ref,
    cos_ref,
    sin_ref,
    dq_ref,
    dpk_ref,
    dpv_ref,
    dtk_ref,
    dtv_ref,
    keys,
    values,
    keys_across,
    key_sums,
    value_sums,
):
    rows = q_ref.shape[0]
    prompt_rows = PROMPT_DEV
    cont = rows - prompt_rows
    prompt_total = pk_ref.shape[0]
    key_total = prompt_total + tk_ref.shape[0]
    stage_pairs(pk_ref, tk_ref, keys)
    stage_pairs(pv_ref, tv_ref, values)
    first_position = place_ref[0]
    odd = place_ref[1]
    factor = ATTN_SCALE * LOG2E
    keys_across[:, :prompt_total] = pk_ref[...].astype(jnp.float32).T.astype(jnp.bfloat16)
    keys_across[:, prompt_total:] = tk_ref[...].astype(jnp.float32).T.astype(jnp.bfloat16)
    key_at = lax.broadcasted_iota(jnp.int32, (prompt_total, prompt_rows), 0)
    row_at = lax.broadcasted_iota(jnp.int32, (prompt_total, prompt_rows), 1)
    prompt_ok = key_at <= row_at + first_position
    tail_at = lax.broadcasted_iota(jnp.int32, (2 * cont, cont), 0)
    cont_at = lax.broadcasted_iota(jnp.int32, (2 * cont, cont), 1)
    tail_ok = ((tail_at < cont) & (odd == 1)) | ((tail_at >= cont) & (tail_at - cont <= cont_at))
    stats = lse_ref[0]
    query_parts = {}
    for own in range(2):
        across = keys_across[64 * own : 64 * own + 64, :]
        for member in range(3):
            head = 3 * own + member
            block, half = head // 2, head % 2
            lanes = slice(block * 128, block * 128 + 128)
            q_own = one_half(q_ref[:, lanes], half == 0)
            do_own = one_half(do_ref[:, lanes], half == 0)
            log_row = stats[head : head + 1, :]
            q_cont, do_cont = q_own[prompt_rows:], do_own[prompt_rows:]
            log_cont = log_row[:, prompt_rows:]
            score = matmul_nt(keys[own], q_cont)
            weight_prompt = jnp.exp2(score[:prompt_total] * factor - log_cont)
            weight_tail = jnp.where(
                tail_ok, jnp.exp2(jnp.minimum(score[prompt_total:] * factor - log_cont, 0.0)), 0.0
            )
            weight = jnp.concatenate([weight_prompt, weight_tail], axis=0)
            change = matmul_nt(values[own], do_cont)
            delta = jnp.sum(weight * change, axis=0, keepdims=True)
            score_grad = (weight * (change - delta)).astype(jnp.bfloat16)
            key_part = matmul(score_grad, q_cont)
            value_part = matmul(weight.astype(jnp.bfloat16), do_cont)
            query_cont = matmul(across, score_grad)
            if member == 0:
                key_sums[own] = key_part
                value_sums[own] = value_part
            else:
                key_sums[own] += key_part
                value_sums[own] += value_part
            q_first, do_first = q_own[:prompt_rows], do_own[:prompt_rows]
            log_first = log_row[:, :prompt_rows]
            score = matmul_nt(keys[own, :prompt_total, :], q_first)
            weight = jnp.where(
                prompt_ok, jnp.exp2(jnp.minimum(score * factor - log_first, 0.0)), 0.0
            )
            change = matmul_nt(values[own, :prompt_total, :], do_first)
            delta = jnp.sum(weight * change, axis=0, keepdims=True)
            score_grad = (weight * (change - delta)).astype(jnp.bfloat16)
            key_sums[own, :prompt_total, :] += matmul(score_grad, q_first)
            value_sums[own, :prompt_total, :] += matmul(weight.astype(jnp.bfloat16), do_first)
            query_first = matmul(across[:, :prompt_total], score_grad)
            query_parts[head] = jnp.concatenate([query_first, query_cont], axis=1)
    for block in range(3):
        lanes = slice(block * 128, block * 128 + 128)
        turned = jnp.concatenate([query_parts[2 * block], query_parts[2 * block + 1]], axis=0)
        flat = turned.T * ATTN_SCALE
        dq_ref[:, lanes] = turn(flat, cos_ref[...], sin_ref[...]).astype(jnp.bfloat16)
    key_pair = fold_halves(key_sums[0], True) + fold_halves(key_sums[1], False)
    key_pair = key_pair * ATTN_SCALE
    value_pair = fold_halves(value_sums[0], True) + fold_halves(value_sums[1], False)
    dpk_ref[...] = key_pair[:prompt_total].astype(jnp.bfloat16)
    dtk_ref[...] = key_pair[prompt_total:]
    dpv_ref[...] = value_pair[:prompt_total].astype(jnp.bfloat16)
    dtv_ref[...] = value_pair[prompt_total:]


def attend_back(place, projected, upstream, prompt_pairs, tail_pairs, stats, cosines, sines):
    rows, width = upstream.shape
    prompt_total = prompt_pairs.shape[0]
    kv_width = KV_HEADS * HEAD
    tail_total = tail_pairs.shape[0]
    pairs = KV_HEADS // 2
    per_pair = width // pairs
    key_total = prompt_total + tail_total
    across = stats[:, :, :8].transpose(0, 2, 1)
    own_rows = pl.BlockSpec((rows, per_pair), lambda p: (0, p))
    prompt_spec = pl.BlockSpec((prompt_total, 128), lambda p: (0, p))
    tail_spec = pl.BlockSpec((tail_total, 128), lambda p: (0, p))
    table = pl.BlockSpec((rows, 128), lambda p: (0, 0))
    return pl.pallas_call(
        attend_back_kernel,
        grid=(pairs,),
        in_specs=[
            pl.BlockSpec(memory_space=pltpu.SMEM),
            own_rows,
            own_rows,
            prompt_spec,
            pl.BlockSpec((prompt_total, 128), lambda p: (0, p + pairs)),
            tail_spec,
            pl.BlockSpec((tail_total, 128), lambda p: (0, p + pairs)),
            pl.BlockSpec((1, 8, rows), lambda p: (p, 0, 0)),
            table,
            table,
        ],
        out_specs=[own_rows, prompt_spec, prompt_spec, tail_spec, tail_spec],
        out_shape=[
            jax.ShapeDtypeStruct((rows, width), jnp.bfloat16),
            jax.ShapeDtypeStruct((prompt_total, kv_width), jnp.bfloat16),
            jax.ShapeDtypeStruct((prompt_total, kv_width), jnp.bfloat16),
            jax.ShapeDtypeStruct((tail_total, kv_width), jnp.float32),
            jax.ShapeDtypeStruct((tail_total, kv_width), jnp.float32),
        ],
        scratch_shapes=[
            pltpu.VMEM((2, key_total, 128), jnp.bfloat16),
            pltpu.VMEM((2, key_total, 128), jnp.bfloat16),
            pltpu.VMEM((128, key_total), jnp.bfloat16),
            pltpu.VMEM((2, key_total, 128), jnp.float32),
            pltpu.VMEM((2, key_total, 128), jnp.float32),
        ],
        compiler_params=pltpu.CompilerParams(vmem_limit_bytes=VMEM_GRANT),
        cost_estimate=pl.CostEstimate(
            flops=rows * width, bytes_accessed=rows * width, transcendentals=0
        ),
        name="attend_back",
    )(
        place,
        projected,
        upstream,
        prompt_pairs,
        prompt_pairs,
        tail_pairs,
        tail_pairs,
        across,
        cosines,
        sines,
    )


def pair_tables(position):
    frequency = ROPE_BASE ** (-jnp.arange(HEAD // 2, dtype=jnp.float32) * 2.0 / HEAD)
    angles = position.astype(jnp.float32)[:, None] * frequency[None, :]
    cosine, sine = jnp.cos(angles), jnp.sin(angles)
    return (
        jnp.concatenate([cosine, cosine, cosine, cosine], axis=1),
        jnp.concatenate([sine, -sine, sine, -sine], axis=1),
    )


def turn(flat, cosines, sines):
    front = lax.broadcasted_iota(jnp.int32, flat.shape, 1) % 64 < 32
    partner = jnp.where(front, pltpu.roll(flat, 96, 1), pltpu.roll(flat, 32, 1))
    return flat * cosines + partner * sines


def project_kernel(turned_blocks, x_ref, w_ref, cos_ref, sin_ref, o_ref):
    made = matmul(x_ref[...], w_ref[...])
    rotates = pl.program_id(0) < turned_blocks
    for lanes in (slice(0, 128), slice(128, 256)):
        part = made[:, lanes]
        o_ref[:, lanes] = jnp.where(
            rotates, turn(part, cos_ref[...], -sin_ref[...]), part
        ).astype(jnp.bfloat16)


def project(normed, weights, cosines, sines):
    rows, width = normed.shape
    columns = (HEADS + 2 * KV_HEADS) * HEAD
    table = pl.BlockSpec((rows, 128), lambda j: (0, 0))
    return pl.pallas_call(
        functools.partial(project_kernel, (HEADS + KV_HEADS) * HEAD // 256),
        grid=(columns // 256,),
        in_specs=[
            pl.BlockSpec((rows, width), lambda j: (0, 0)),
            pl.BlockSpec((width, 256), lambda j: (0, j)),
            table,
            table,
        ],
        out_specs=pl.BlockSpec((rows, 256), lambda j: (0, j)),
        out_shape=jax.ShapeDtypeStruct((rows, columns), jnp.bfloat16),
        compiler_params=pltpu.CompilerParams(vmem_limit_bytes=VMEM_GRANT),
        cost_estimate=pl.CostEstimate(
            flops=2 * rows * width * columns, bytes_accessed=2 * width * columns, transcendentals=0
        ),
        name="project",
    )(normed, weights, cosines, sines)


def expert_rows(first, x, g, codes, up_ref, down_ref, router_ref, dgu_ref, act_ref):
    local_experts, hidden = down_ref.shape[0], down_ref.shape[1]
    logits = matmul(x, router_ref[...])
    gates = gates_of(logits, codes)
    kept = codes > 1.5
    lane = lax.broadcasted_iota(jnp.int32, logits.shape, 1)
    placed = jnp.zeros(logits.shape, jnp.float32)
    total = None
    for local in range(local_experts):
        mine = (lane == first + local) & kept
        weight = jnp.sum(jnp.where(mine, gates, 0.0), axis=1, keepdims=True)
        made = matmul(x, up_ref[local])
        act_grad = matmul_nt(g, down_ref[local])
        gate_part, up_part = made[:, :hidden], made[:, hidden:]
        sigma = jax.nn.sigmoid(gate_part)
        silu = gate_part * sigma
        acted = (silu * up_part).astype(jnp.bfloat16).astype(jnp.float32)
        act_ref[local] = (weight * acted).astype(jnp.bfloat16)
        pair_grad = RESIDUAL * jnp.sum(acted * act_grad, axis=1, keepdims=True)
        placed = jnp.where(mine, pair_grad, placed)
        scaled = (RESIDUAL * weight) * act_grad
        gate_grad = scaled * up_part * sigma * (1.0 + gate_part * (1.0 - sigma))
        both = jnp.concatenate([gate_grad, scaled * silu], axis=1).astype(jnp.bfloat16)
        dgu_ref[local] = both
        part = matmul_nt(both, up_ref[local])
        total = part if total is None else total + part
    high = placed.astype(jnp.bfloat16).astype(jnp.float32)
    rest = pltpu.roll(placed - high, 64, 1)
    return jnp.concatenate([total, high + rest], axis=1).astype(jnp.bfloat16)


def experts_kernel(
    place_ref, x_ref, g_ref, up_ref, down_ref, router_ref, codes_ref, dx_ref, dgu_ref, act_ref
):
    dx_ref[...] = expert_rows(
        place_ref[2],
        x_ref[...],
        g_ref[...],
        codes_ref[...].astype(jnp.float32),
        up_ref,
        down_ref,
        router_ref,
        dgu_ref,
        act_ref,
    )


def experts(place, rows_in, rows_grad, gate_up, down, weights, codes):
    total, width = rows_in.shape
    local_experts, hidden = down.shape[0], down.shape[1]
    step = 256
    whole = pl.Buffered(1)
    return pl.pallas_call(
        experts_kernel,
        grid=(total // step,),
        in_specs=[
            pl.BlockSpec(memory_space=pltpu.SMEM),
            pl.BlockSpec((step, width), lambda i: (i, 0)),
            pl.BlockSpec((step, width), lambda i: (i, 0)),
            pl.BlockSpec(gate_up.shape, lambda i: (0, 0, 0), pipeline_mode=whole),
            pl.BlockSpec(down.shape, lambda i: (0, 0, 0), pipeline_mode=whole),
            pl.BlockSpec((width, 128), lambda i: (0, 0), pipeline_mode=whole),
            pl.BlockSpec((step, 128), lambda i: (i, 0)),
        ],
        out_specs=[
            pl.BlockSpec((step, width + 128), lambda i: (i, 0)),
            pl.BlockSpec((local_experts, step, 2 * hidden), lambda i: (0, i, 0)),
            pl.BlockSpec((local_experts, step, hidden), lambda i: (0, i, 0)),
        ],
        out_shape=[
            jax.ShapeDtypeStruct((total, width + 128), jnp.bfloat16),
            jax.ShapeDtypeStruct((local_experts, total, 2 * hidden), jnp.bfloat16),
            jax.ShapeDtypeStruct((local_experts, total, hidden), jnp.bfloat16),
        ],
        compiler_params=pltpu.CompilerParams(vmem_limit_bytes=VMEM_GRANT),
        cost_estimate=pl.CostEstimate(
            flops=10 * total * width * local_experts * hidden,
            bytes_accessed=16 * total * width,
            transcendentals=total * local_experts * hidden,
        ),
        name="experts",
    )(place, rows_in, rows_grad, gate_up, down, weights, codes)


def flipped(index, step):
    core, across, along = index % 2, index // 2 % 2, index // 4
    return (
        index
        + (step % 2) * (1 - 2 * core)
        + 2 * (step // 2 % 2) * (1 - 2 * across)
        + 4 * (step // 4) * (1 - 2 * along)
    )


def gather_weights_kernel(
    query_hbm,
    key_hbm,
    value_hbm,
    out_hbm,
    fused_hbm,
    piece_hbm,
    local_sem,
    line_send,
    plane_send,
    pass_send,
    recv_sem,
    piece_send,
    piece_recv,
):
    level, me = lax.axis_index("dp"), lax.axis_index("expert")
    shard = query_hbm.shape[0]
    part = piece_hbm.shape[0] // 4
    q_width, kv_width = query_hbm.shape[1], key_hbm.shape[1]
    barrier = pltpu.get_barrier_semaphore()
    plane_steps, line_steps = (2, 4, 6, 1), (1, 2, 3)
    for step in plane_steps:
        pl.semaphore_signal(
            barrier, inc=1, device_id={"expert": flipped(me, step)}, device_id_type=MESH_ID
        )
    for step in line_steps:
        pl.semaphore_signal(
            barrier, inc=1, device_id={"dp": flipped(level, step)}, device_id_type=MESH_ID
        )
    own = pl.ds(pl.multiple_of(me * part, part), part)

    def rows(line_step, plane_step):
        start = flipped(level, line_step) * shard + flipped(me, plane_step) * part
        return fused_hbm.at[pl.ds(pl.multiple_of(start, part), part)]

    mine = pl.ds(pl.multiple_of(level * shard + me * part, part), part)
    starts = (
        pltpu.make_async_copy(
            query_hbm.at[own], fused_hbm.at[mine, pl.ds(0, q_width)], local_sem.at[0]
        ),
        pltpu.make_async_copy(
            key_hbm.at[own], fused_hbm.at[mine, pl.ds(q_width, kv_width)], local_sem.at[1]
        ),
        pltpu.make_async_copy(
            value_hbm.at[own],
            fused_hbm.at[mine, pl.ds(q_width + kv_width, kv_width)],
            local_sem.at[2],
        ),
        pltpu.make_async_copy(
            out_hbm.at[own],
            piece_hbm.at[pl.ds(pl.multiple_of(level * part, part), part)],
            local_sem.at[3],
        ),
    )

    def along(step):
        return pltpu.make_async_remote_copy(
            src_ref=rows(0, 0),
            dst_ref=rows(0, 0),
            send_sem=line_send.at[step],
            recv_sem=recv_sem.at[step, 0],
            device_id={"dp": flipped(level, step)},
            device_id_type=MESH_ID,
        )

    def along_out(step):
        place = piece_hbm.at[pl.ds(pl.multiple_of(level * part, part), part)]
        return pltpu.make_async_remote_copy(
            src_ref=place,
            dst_ref=place,
            send_sem=piece_send.at[step],
            recv_sem=piece_recv.at[step],
            device_id={"dp": flipped(level, step)},
            device_id_type=MESH_ID,
        )

    def across(line_step, step):
        return pltpu.make_async_remote_copy(
            src_ref=rows(line_step, 0),
            dst_ref=rows(line_step, 0),
            send_sem=plane_send.at[line_step, step],
            recv_sem=recv_sem.at[line_step, step],
            device_id={"expert": flipped(me, step)},
            device_id_type=MESH_ID,
        )

    def pass_on(line_step, step):
        return pltpu.make_async_remote_copy(
            src_ref=rows(line_step, step),
            dst_ref=rows(line_step, step),
            send_sem=pass_send.at[line_step, step],
            recv_sem=recv_sem.at[line_step, step + 1],
            device_id={"expert": flipped(me, 1)},
            device_id_type=MESH_ID,
        )

    for copy in starts:
        copy.start()
    for copy in starts[:3]:
        copy.wait()
    pl.semaphore_wait(barrier, len(plane_steps) + len(line_steps))
    for step in line_steps:
        along(step).start()
    for step in plane_steps:
        across(0, step).start()
    starts[3].wait()
    for step in line_steps:
        along_out(step).start()

    def wait_level(line_step, carry):
        along(line_step).wait_recv()
        for step in plane_steps:
            across(line_step, step).start()
        return carry

    def pass_level(line_step, carry):
        for step in (2, 4, 6):
            across(line_step, step).wait_recv()
            pass_on(line_step, step).start()
        return carry

    def last_level(line_step, carry):
        for step in (1, 3, 5, 7):
            across(line_step, step).wait_recv()
        for step in plane_steps:
            across(line_step, step).wait_send()
        for step in (2, 4, 6):
            pass_on(line_step, step).wait_send()
        return carry

    wait_level(1, 0)
    pass_level(0, 0)
    wait_level(2, 0)
    pass_level(1, 0)
    wait_level(3, 0)
    pass_level(2, 0)
    pass_level(3, 0)
    lax.fori_loop(0, 4, last_level, 0)
    for step in line_steps:
        along(step).wait_send()
        along_out(step).wait()


def gather_weights(query_proj, key_proj, value_proj, out_proj):
    shard = query_proj.shape[0]
    columns = query_proj.shape[1] + 2 * key_proj.shape[1]
    anywhere = pl.BlockSpec(memory_space=pl.ANY)
    dma = pltpu.SemaphoreType.DMA
    return pl.pallas_call(
        gather_weights_kernel,
        in_specs=[anywhere] * 4,
        out_specs=[anywhere] * 2,
        out_shape=[
            jax.ShapeDtypeStruct((4 * shard, columns), jnp.bfloat16),
            jax.ShapeDtypeStruct((shard // 2, out_proj.shape[1]), jnp.bfloat16),
        ],
        scratch_shapes=[
            dma((4,)),
            dma((4,)),
            dma((4, 8)),
            dma((4, 8)),
            dma((4, 8)),
            dma((4,)),
            dma((4,)),
        ],
        compiler_params=pltpu.CompilerParams(
            collective_id=2, has_side_effects=True, vmem_limit_bytes=1024 * 1024
        ),
        cost_estimate=pl.CostEstimate(
            flops=0, bytes_accessed=16 * shard * columns, transcendentals=0
        ),
        name="gather_weights",
    )(query_proj, key_proj, value_proj, out_proj)


def share_pairs_kernel(
    rows_hbm, prompt_hbm, tail_hbm, local_sem, tail_send, tail_recv, send_sem, pass_sem, recv_sem
):
    me = lax.axis_index("expert")
    columns = prompt_hbm.shape[1]
    count = prompt_hbm.shape[0] // 8
    cont = tail_hbm.shape[0] // 2
    pairs_at = pl.ds(rows_hbm.shape[1] - columns, columns)
    barrier = pltpu.get_barrier_semaphore()
    for step in (1, 2, 4, 6):
        pl.semaphore_signal(
            barrier, inc=1, device_id={"expert": flipped(me, step)}, device_id_type=MESH_ID
        )

    def block(step):
        return prompt_hbm.at[pl.ds(pl.multiple_of(flipped(me, step) * count, count), count)]

    own_prompt = rows_hbm.at[pl.ds(0, count), pairs_at]
    own_cont = rows_hbm.at[pl.ds(count, cont), pairs_at]
    local = (
        pltpu.make_async_copy(own_prompt, block(0), local_sem.at[0]),
        pltpu.make_async_copy(own_cont, tail_hbm.at[pl.ds(cont, cont)], local_sem.at[1]),
    )
    tail = pltpu.make_async_remote_copy(
        src_ref=own_cont,
        dst_ref=tail_hbm.at[pl.ds(0, cont)],
        send_sem=tail_send,
        recv_sem=tail_recv,
        device_id={"expert": flipped(me, 1)},
        device_id_type=MESH_ID,
    )

    def send(step):
        return pltpu.make_async_remote_copy(
            src_ref=own_prompt,
            dst_ref=block(0),
            send_sem=send_sem.at[step],
            recv_sem=recv_sem.at[step],
            device_id={"expert": flipped(me, step)},
            device_id_type=MESH_ID,
        )

    def pass_on(step):
        return pltpu.make_async_remote_copy(
            src_ref=block(step),
            dst_ref=block(step),
            send_sem=pass_sem.at[step],
            recv_sem=recv_sem.at[step + 1],
            device_id={"expert": flipped(me, 1)},
            device_id_type=MESH_ID,
        )

    for copy in local:
        copy.start()
    pl.semaphore_wait(barrier, 4)
    for step in (2, 4, 6, 1):
        send(step).start()
    tail.start()
    for step in (2, 4, 6):
        send(step).wait_recv()
        pass_on(step).start()
    for step in (1, 3, 5, 7):
        send(step).wait_recv()
    for step in (1, 2, 4, 6):
        send(step).wait_send()
    for step in (2, 4, 6):
        pass_on(step).wait_send()
    tail.wait()
    for copy in local:
        copy.wait()


def share_pairs(projected):
    rows = projected.shape[0]
    columns = 2 * KV_HEADS * HEAD
    anywhere = pl.BlockSpec(memory_space=pl.ANY)
    dma = pltpu.SemaphoreType.DMA
    return pl.pallas_call(
        share_pairs_kernel,
        in_specs=[anywhere],
        out_specs=[anywhere] * 2,
        out_shape=[
            jax.ShapeDtypeStruct((8 * PROMPT_DEV, columns), jnp.bfloat16),
            jax.ShapeDtypeStruct((2 * (rows - PROMPT_DEV), columns), jnp.bfloat16),
        ],
        scratch_shapes=[dma((2,)), dma, dma, dma((8,)), dma((8,)), dma((8,))],
        compiler_params=pltpu.CompilerParams(
            collective_id=3, has_side_effects=True, vmem_limit_bytes=1024 * 1024
        ),
        cost_estimate=pl.CostEstimate(
            flops=0, bytes_accessed=32 * PROMPT_DEV * columns, transcendentals=0
        ),
        name="share_pairs",
    )(projected)


def line_sum_kernel(
    count,
    mine_hbm,
    total_hbm,
    mine,
    partial,
    result,
    wide,
    load_sem,
    up_send,
    up_recv,
    down_send,
    down_recv,
    store_sem,
):
    chunks = mine.shape[0]
    at = lax.axis_index("dp")
    last = count - 1
    barrier = pltpu.get_barrier_semaphore()

    @pl.when(at > 0)
    def _():
        pl.semaphore_signal(barrier, inc=1, device_id={"dp": at - 1}, device_id_type=MESH_ID)

    @pl.when(at < last)
    def _():
        pl.semaphore_signal(barrier, inc=1, device_id={"dp": at + 1}, device_id_type=MESH_ID)

    def load(chunk):
        return pltpu.make_async_copy(mine_hbm.at[chunk], mine.at[chunk], load_sem.at[chunk])

    def upward(chunk):
        return pltpu.make_async_remote_copy(
            src_ref=mine.at[chunk],
            dst_ref=partial.at[chunk],
            send_sem=up_send.at[chunk],
            recv_sem=up_recv.at[chunk],
            device_id={"dp": at + 1},
            device_id_type=MESH_ID,
        )

    def downward(source, chunk):
        return pltpu.make_async_remote_copy(
            src_ref=source.at[chunk],
            dst_ref=result.at[chunk],
            send_sem=down_send.at[chunk],
            recv_sem=down_recv.at[chunk],
            device_id={"dp": at - 1},
            device_id_type=MESH_ID,
        )

    def store(slot, chunk):
        return pltpu.make_async_copy(wide.at[slot], total_hbm.at[chunk], store_sem.at[slot])

    lax.fori_loop(0, chunks, lambda chunk, c: (load(chunk).start(), c)[1], 0)
    pl.semaphore_wait(barrier, jnp.where(at > 0, 1, 0) + jnp.where(at < last, 1, 0))
    lag = 2 * (last - at) + jnp.where(at < last, 2, 0)

    def finish(source, done):
        slot = lax.rem(done, 2)

        @pl.when(done >= 2)
        def _():
            store(slot, done - 2).wait()

        wide[slot] = source[done].astype(jnp.float32)
        store(slot, done).start()

    def tick(step, carry):
        @pl.when(step < chunks)
        def _():
            load(step).wait()

            @pl.when(at > 0)
            def _():
                upward(step).wait_recv()
                mine[step] = (
                    mine[step].astype(jnp.float32) + partial[step].astype(jnp.float32)
                ).astype(jnp.bfloat16)

            @pl.when(at < last)
            def _():
                upward(step).start()

        done = step - lag

        @pl.when((done >= 0) & (done < chunks))
        def _():
            @pl.when(at == last)
            def _():
                downward(mine, done).start()
                finish(mine, done)

            @pl.when(at < last)
            def _():
                downward(result, done).wait_recv()

                @pl.when(at > 0)
                def _():
                    downward(result, done).start()

                finish(result, done)

        return carry

    lax.fori_loop(0, chunks + 2 * last + 2, tick, 0)
    for late in (chunks - 2, chunks - 1):
        store(late % 2, late).wait()

    def drain(chunk, carry):
        @pl.when(at < last)
        def _():
            upward(chunk).wait_send()

        @pl.when(at > 0)
        def _():
            downward(result, chunk).wait_send()

        return carry

    lax.fori_loop(0, chunks, drain, 0)


def line_sum(count, number, values):
    shape = values.shape
    chunks = shape[0]
    dma = pltpu.SemaphoreType.DMA
    return pl.pallas_call(
        functools.partial(line_sum_kernel, count),
        in_specs=[pl.BlockSpec(memory_space=pl.ANY)],
        out_specs=pl.BlockSpec(memory_space=pl.ANY),
        out_shape=jax.ShapeDtypeStruct(shape, jnp.float32),
        scratch_shapes=[
            pltpu.VMEM(shape, jnp.bfloat16),
            pltpu.VMEM(shape, jnp.bfloat16),
            pltpu.VMEM(shape, jnp.bfloat16),
            pltpu.VMEM((2,) + shape[1:], jnp.float32),
            dma((chunks,)),
            dma((chunks,)),
            dma((chunks,)),
            dma((chunks,)),
            dma((chunks,)),
            dma((2,)),
        ],
        compiler_params=pltpu.CompilerParams(
            collective_id=number, has_side_effects=True, vmem_limit_bytes=VMEM_GRANT
        ),
        cost_estimate=pl.CostEstimate(
            flops=0, bytes_accessed=60 * values.size, transcendentals=0
        ),
        name="line_sum",
    )(values)


def line_scatter_kernel(
    parts_hbm, sum_ref, landed, local_sem, send_sem, recv_sem
):
    level = lax.axis_index("dp")
    rows = sum_ref.shape[0]
    barrier = pltpu.get_barrier_semaphore()
    for step in (1, 2, 3):
        pl.semaphore_signal(
            barrier, inc=1, device_id={"dp": flipped(level, step)}, device_id_type=MESH_ID
        )

    def part(step):
        start = flipped(level, step) * rows
        return parts_hbm.at[pl.ds(pl.multiple_of(start, rows), rows)]

    def send(step):
        return pltpu.make_async_remote_copy(
            src_ref=part(step),
            dst_ref=landed.at[step],
            send_sem=send_sem.at[step],
            recv_sem=recv_sem.at[step],
            device_id={"dp": flipped(level, step)},
            device_id_type=MESH_ID,
        )

    own = pltpu.make_async_copy(part(0), landed.at[0], local_sem)
    own.start()
    pl.semaphore_wait(barrier, 3)
    for step in (2, 3, 1):
        send(step).start()
    own.wait()
    for step in (1, 2, 3):
        send(step).wait_recv()
    total = landed[0].astype(jnp.float32) + landed[1].astype(jnp.float32)
    total += landed[2].astype(jnp.float32)
    total += landed[3].astype(jnp.float32)
    sum_ref[...] = total.astype(jnp.bfloat16)
    for step in (1, 2, 3):
        send(step).wait_send()


def line_scatter(parts):
    rows, columns = parts.shape[0] // 4, parts.shape[1]
    dma = pltpu.SemaphoreType.DMA
    return pl.pallas_call(
        line_scatter_kernel,
        in_specs=[pl.BlockSpec(memory_space=pl.ANY)],
        out_specs=pl.BlockSpec(memory_space=pltpu.VMEM),
        out_shape=jax.ShapeDtypeStruct((rows, columns), jnp.bfloat16),
        scratch_shapes=[pltpu.VMEM((4, rows, columns), jnp.bfloat16), dma, dma((4,)), dma((4,))],
        compiler_params=pltpu.CompilerParams(
            collective_id=4, has_side_effects=True, vmem_limit_bytes=16 * 1024 * 1024
        ),
        cost_estimate=pl.CostEstimate(
            flops=0, bytes_accessed=100 * rows * columns, transcendentals=0
        ),
        name="line_scatter",
    )(parts)


def return_pairs_kernel(
    key_ref,
    value_ref,
    tail_key_ref,
    tail_value_ref,
    cos_ref,
    sin_ref,
    low_ref,
    tail_out,
    tail_in,
    pairs_in,
    joined,
    last_in,
    tail_send,
    tail_recv,
    pair_send,
    pair_recv,
    last_send,
    last_recv,
):
    me = lax.axis_index("expert")
    count = pairs_in.shape[2]
    kv_width = key_ref.shape[1]
    cont = tail_out.shape[0]
    barrier = pltpu.get_barrier_semaphore()
    for step in (1, 2, 4, 6):
        pl.semaphore_signal(
            barrier, inc=1, device_id={"expert": flipped(me, step)}, device_id_type=MESH_ID
        )

    def block_of(step):
        return pl.ds(pl.multiple_of(flipped(me, step) * count, count), count)

    sources = (key_ref, value_ref)

    def remote(source, target, sent, landed, step):
        return pltpu.make_async_remote_copy(
            src_ref=source,
            dst_ref=target,
            send_sem=sent,
            recv_sem=landed,
            device_id={"expert": flipped(me, step)},
            device_id_type=MESH_ID,
        )

    def to_sibling(half, which):
        return remote(
            sources[which].at[block_of(2 * half + 1)],
            pairs_in.at[half, which],
            pair_send.at[half, which],
            pair_recv.at[half, which],
            1,
        )

    def to_owner(half, which):
        return remote(
            joined.at[half, which],
            last_in.at[half, which],
            last_send.at[half, which],
            last_recv.at[half, which],
            2 * half,
        )

    tail = remote(tail_out, tail_in, tail_send, tail_recv, 1)
    pl.semaphore_wait(barrier, 4)
    for half in (1, 2, 3, 0):
        for which in range(2):
            to_sibling(half, which).start()
    tail_out[:, :kv_width] = tail_key_ref[:cont].astype(jnp.bfloat16)
    tail_out[:, kv_width:] = tail_value_ref[:cont].astype(jnp.bfloat16)
    tail.start()
    for half in (3, 1, 2):
        for which in range(2):
            to_sibling(half, which).wait_recv()
            joined[half, which] = (
                sources[which][block_of(2 * half), :].astype(jnp.float32)
                + pairs_in[half, which].astype(jnp.float32)
            ).astype(jnp.bfloat16)
            to_owner(half, which).start()
    tail.wait_recv()
    blocks = kv_width // 128
    for block in range(blocks):
        lanes = slice(block * 128, block * 128 + 128)
        values = slice(kv_width + block * 128, kv_width + block * 128 + 128)
        grown = tail_key_ref[cont:, lanes] + tail_in[:, lanes].astype(jnp.float32)
        low_ref[count:, lanes] = turn(grown, cos_ref[count:], sin_ref[count:]).astype(jnp.bfloat16)
        grown = tail_value_ref[cont:, lanes] + tail_in[:, values].astype(jnp.float32)
        low_ref[count:, values] = grown.astype(jnp.bfloat16)
    totals = []
    for which in range(2):
        to_sibling(0, which).wait_recv()
        totals.append(
            sources[which][block_of(0), :].astype(jnp.float32)
            + pairs_in[0, which].astype(jnp.float32)
        )
    for half in (1, 2, 3):
        for which in range(2):
            to_owner(half, which).wait_recv()
            totals[which] = totals[which] + last_in[half, which].astype(jnp.float32)
    for block in range(blocks):
        lanes = slice(block * 128, block * 128 + 128)
        low_ref[:count, lanes] = turn(
            totals[0][:, lanes], cos_ref[:count], sin_ref[:count]
        ).astype(jnp.bfloat16)
    low_ref[:count, kv_width:] = totals[1].astype(jnp.bfloat16)
    tail.wait_send()
    for half in range(4):
        for which in range(2):
            to_sibling(half, which).wait_send()
    for half in (1, 2, 3):
        for which in range(2):
            to_owner(half, which).wait_send()


def return_pairs(key_part, value_part, tail_keys, tail_values, cosines, sines):
    kv_width = key_part.shape[1]
    count, cont = PROMPT_DEV, tail_keys.shape[0] // 2
    resident = pl.BlockSpec(memory_space=pltpu.VMEM)
    dma = pltpu.SemaphoreType.DMA
    pieces = pltpu.VMEM((4, 2, count, kv_width), jnp.bfloat16)
    rows = pltpu.VMEM((cont, 2 * kv_width), jnp.bfloat16)
    return pl.pallas_call(
        return_pairs_kernel,
        in_specs=[resident] * 6,
        out_specs=resident,
        out_shape=jax.ShapeDtypeStruct((count + cont, 2 * kv_width), jnp.bfloat16),
        scratch_shapes=[
            rows,
            rows,
            pieces,
            pieces,
            pieces,
            dma,
            dma,
            dma((4, 2)),
            dma((4, 2)),
            dma((4, 2)),
            dma((4, 2)),
        ],
        compiler_params=pltpu.CompilerParams(
            collective_id=5, has_side_effects=True, vmem_limit_bytes=24 * 1024 * 1024
        ),
        cost_estimate=pl.CostEstimate(flops=0, bytes_accessed=8 * 1024 * 1024, transcendentals=0),
        name="return_pairs",
    )(key_part, value_part, tail_keys, tail_values, cosines, sines)


def gathering_experts_kernel(
    own_hbm,
    g_hbm,
    up_ref,
    down_ref,
    router_ref,
    dx_hbm,
    dgu_hbm,
    act_hbm,
    x_hbm,
    rows,
    grads,
    dx_out,
    dgu_out,
    act_out,
    own_sem,
    send_sem,
    pass_sem,
    recv_sem,
    grad_sem,
    x_sem,
    dx_sem,
    dgu_sem,
    act_sem,
):
    me = lax.axis_index("expert")
    local_experts = down_ref.shape[0]
    steps, count = rows.shape[0], rows.shape[1]
    barrier = pltpu.get_barrier_semaphore()
    for step in (1, 2, 4):
        pl.semaphore_signal(
            barrier, inc=1, device_id={"expert": flipped(me, step)}, device_id_type=MESH_ID
        )

    def block_of(step):
        return pl.ds(pl.multiple_of(flipped(me, step) * count, count), count)

    def grad_load(step):
        return pltpu.make_async_copy(
            g_hbm.at[block_of(step)], grads.at[step % 2], grad_sem.at[step % 2]
        )

    half_count = count // 2
    top, bottom = pl.ds(0, half_count), pl.ds(half_count, half_count)

    def remote(source, target, sent, landed, step):
        return pltpu.make_async_remote_copy(
            src_ref=source,
            dst_ref=target,
            send_sem=sent,
            recv_sem=landed,
            device_id={"expert": flipped(me, step)},
            device_id_type=MESH_ID,
        )

    def send(step):
        return remote(rows.at[0], rows.at[step], send_sem.at[step], recv_sem.at[step], step)

    def pass_on(step):
        return remote(
            rows.at[step], rows.at[step + 1], pass_sem.at[step], recv_sem.at[step + 1], 1
        )

    def relay_top():
        return remote(rows.at[2, top], rows.at[6, top], send_sem.at[6], recv_sem.at[6], 4)

    def relay_bottom():
        return remote(rows.at[4, bottom], rows.at[6, bottom], send_sem.at[7], recv_sem.at[0], 2)

    def x_store(step):
        return pltpu.make_async_copy(
            rows.at[step, :, pl.ds(0, x_hbm.shape[1])], x_hbm.at[block_of(step)], x_sem.at[step]
        )

    def stores(step):
        slot = step % 2
        return (
            pltpu.make_async_copy(dx_out.at[slot], dx_hbm.at[block_of(step)], dx_sem.at[slot]),
            pltpu.make_async_copy(dgu_out.at[slot], dgu_hbm.at[:, block_of(step)], dgu_sem.at[slot]),
            pltpu.make_async_copy(act_out.at[slot], act_hbm.at[:, block_of(step)], act_sem.at[slot]),
        )

    own_load = pltpu.make_async_copy(own_hbm, rows.at[0], own_sem)
    own_load.start()
    grad_load(0).start()
    own_load.wait()
    pl.semaphore_wait(barrier, 3)
    for step in (2, 4, 1):
        send(step).start()

    def work(step, carry):
        @pl.when(step == 2)
        def _():
            send(2).wait_recv()
            relay_top().start()
            pass_on(2).start()
            send(4).wait_recv()
            relay_bottom().start()
            pass_on(4).start()

        @pl.when(step == 6)
        def _():
            relay_top().wait_recv()
            relay_bottom().wait_recv()
            pass_on(6).start()

        @pl.when(step % 2 == 1)
        def _():
            send(step).wait_recv()

        x_store(step).start()

        @pl.when(step + 1 < steps)
        def _():
            grad_load(step + 1).start()

        grad_load(step).wait()
        slot = step % 2

        @pl.when(step >= 2)
        def _():
            for copy in stores(step - 2):
                copy.wait()

        dx_out[slot] = expert_rows(
            me * local_experts,
            rows[step, :, : x_hbm.shape[1]],
            grads[slot],
            rows[step, :, x_hbm.shape[1] :].astype(jnp.float32),
            up_ref,
            down_ref,
            router_ref,
            dgu_out.at[slot],
            act_out.at[slot],
        )
        for copy in stores(step):
            copy.start()
        return carry

    lax.fori_loop(0, steps, work, 0)
    for step in (steps - 2, steps - 1):
        for copy in stores(step):
            copy.wait()
    for step in (1, 2, 4):
        send(step).wait_send()
    relay_top().wait_send()
    relay_bottom().wait_send()
    for step in (2, 4, 6):
        pass_on(step).wait_send()
    for step in range(steps):
        x_store(step).wait()


def gathering_experts(own_rows, rows_grad, gate_up, down, weights):
    count = own_rows.shape[0]
    total, width = rows_grad.shape
    steps = total // count
    local_experts, hidden = down.shape[0], down.shape[1]
    resident = pl.BlockSpec(memory_space=pltpu.VMEM)
    anywhere = pl.BlockSpec(memory_space=pl.ANY)
    dma = pltpu.SemaphoreType.DMA
    return pl.pallas_call(
        gathering_experts_kernel,
        in_specs=[anywhere, anywhere, resident, resident, resident],
        out_specs=[anywhere] * 4,
        out_shape=[
            jax.ShapeDtypeStruct((total, width + 128), jnp.bfloat16),
            jax.ShapeDtypeStruct((local_experts, total, 2 * hidden), jnp.bfloat16),
            jax.ShapeDtypeStruct((local_experts, total, hidden), jnp.bfloat16),
            jax.ShapeDtypeStruct((total, width), jnp.bfloat16),
        ],
        scratch_shapes=[
            pltpu.VMEM((steps, count, width + 128), jnp.bfloat16),
            pltpu.VMEM((2, count, width), jnp.bfloat16),
            pltpu.VMEM((2, count, width + 128), jnp.bfloat16),
            pltpu.VMEM((2, local_experts, count, 2 * hidden), jnp.bfloat16),
            pltpu.VMEM((2, local_experts, count, hidden), jnp.bfloat16),
            dma,
            dma((steps,)),
            dma((steps,)),
            dma((steps,)),
            dma((2,)),
            dma((steps,)),
            dma((2,)),
            dma((2,)),
            dma((2,)),
        ],
        compiler_params=pltpu.CompilerParams(
            collective_id=1, has_side_effects=True, vmem_limit_bytes=VMEM_GRANT
        ),
        cost_estimate=pl.CostEstimate(
            flops=10 * total * width * local_experts * hidden,
            bytes_accessed=16 * total * width,
            transcendentals=total * local_experts * hidden,
        ),
        name="gathering_experts",
    )(own_rows, rows_grad, gate_up, down, weights)


def shares_kernel(act_ref, down_ref, o_ref):
    total = matmul(act_ref[0], down_ref[0])
    for local in range(1, down_ref.shape[0]):
        total += matmul(act_ref[local], down_ref[local])
    o_ref[...] = total.astype(jnp.bfloat16)


def moe_shares(act, down):
    local_experts, total, hidden = act.shape
    width = down.shape[2]
    step = 512
    return pl.pallas_call(
        shares_kernel,
        grid=(total // step,),
        in_specs=[
            pl.BlockSpec((local_experts, step, hidden), lambda i: (0, i, 0)),
            pl.BlockSpec(down.shape, lambda i: (0, 0, 0)),
        ],
        out_specs=pl.BlockSpec((step, width), lambda i: (i, 0)),
        out_shape=jax.ShapeDtypeStruct((total, width), jnp.bfloat16),
        compiler_params=pltpu.CompilerParams(vmem_limit_bytes=VMEM_GRANT),
        cost_estimate=pl.CostEstimate(
            flops=total * width, bytes_accessed=total * width, transcendentals=0
        ),
        name="moe_shares",
    )(act, down)


def dense_grads_kernel(
    normed_ref, ffn_ref, att_ref, right_ref, out_right_ref, extra_ref, o_ref, *, mixed
):
    block = pl.program_id(0)

    @pl.when(block < mixed)
    def _():
        o_ref[...] = matmul(normed_ref[...], right_ref[...]).astype(jnp.bfloat16)

    @pl.when(block == mixed)
    def _():
        o_ref[:, :256] = matmul(normed_ref[...], right_ref[:, :256]).astype(jnp.bfloat16)
        o_ref[:, 256:] = (matmul(ffn_ref[...], right_ref[:, 256:]) + extra_ref[...]).astype(
            jnp.bfloat16
        )

    @pl.when(block > mixed)
    def _():
        o_ref[...] = matmul(att_ref[...], out_right_ref[...]).astype(jnp.bfloat16)


def dense_weight_grads(normed, ffn_in, attended, right, out_right, extra):
    features, rows = normed.shape
    mixed = right.shape[1] // 384 - 1
    columns = right.shape[1] + out_right.shape[1]
    whole = pl.BlockSpec((features, rows), lambda j: (0, 0))
    return pl.pallas_call(
        functools.partial(dense_grads_kernel, mixed=mixed),
        grid=(columns // 384,),
        in_specs=[
            whole,
            whole,
            whole,
            pl.BlockSpec((rows, 384), lambda j: (0, jnp.minimum(j, mixed))),
            pl.BlockSpec((rows, 384), lambda j: (0, jnp.maximum(j - mixed - 1, 0))),
            pl.BlockSpec((features, 128), lambda j: (0, 0)),
        ],
        out_specs=pl.BlockSpec((features, 384), lambda j: (0, j)),
        out_shape=jax.ShapeDtypeStruct((features, columns), jnp.bfloat16),
        compiler_params=pltpu.CompilerParams(vmem_limit_bytes=VMEM_GRANT),
        cost_estimate=pl.CostEstimate(
            flops=2 * features * rows * columns,
            bytes_accessed=2 * features * columns,
            transcendentals=0,
        ),
        name="dense_weight_grads",
    )(normed, ffn_in, attended, right, out_right, extra)


def on_device(
    layer_in,
    grad_out,
    attn_gain,
    query_proj,
    key_proj,
    value_proj,
    out_proj,
    ffn_gain,
    router_proj,
    gate_up,
    down_proj,
    routes,
    drop_rank,
):
    tok_rows, width = layer_in.shape
    local_experts = gate_up.shape[0]
    hidden_units = down_proj.shape[1]
    top_count = routes.shape[1]
    owner_count = lax.axis_size("expert")
    owner_index = lax.axis_index("expert")
    expert_total = local_experts * owner_count
    capacity = 5 * tok_rows * top_count // (4 * expert_total)
    prompt_rows = PROMPT_DEV
    half_rows = tok_rows - prompt_rows
    prompt_total = prompt_rows * owner_count
    head_size = HEAD
    kv_heads = KV_HEADS
    kv_width = kv_heads * head_size
    dp_count = lax.axis_size("dp")
    shard_rows = query_proj.shape[0]
    piece_rows = shard_rows // owner_count

    def in_order(pieces):
        columns = pieces.shape[1]
        pieces = pieces.reshape(owner_count, dp_count, piece_rows, columns)
        return pieces.transpose(1, 0, 2, 3).reshape(dp_count * shard_rows, columns)

    def whole_of(shard):
        piece = lax.dynamic_slice_in_dim(shard, owner_index * piece_rows, piece_rows, 0)
        piece = lax.all_gather(piece, "dp", axis=0, tiled=True)
        return in_order(lax.all_gather(piece, "expert", axis=0, tiled=True))

    extras = jnp.concatenate(
        [
            router_proj,
            attn_gain[:, None],
            ffn_gain[:, None],
            jnp.zeros((shard_rows, 126 - router_proj.shape[1]), jnp.bfloat16),
        ],
        axis=1,
    )
    small_plane = owner_count == 8 and dp_count == 4
    if small_plane:
        fused, out_piece = gather_weights(query_proj, key_proj, value_proj, out_proj)
        out_piece = lax.all_gather(out_piece, "expert", axis=0, tiled=True)
        full_out = in_order(out_piece)
    else:
        fused = whole_of(jnp.concatenate([query_proj, key_proj, value_proj], axis=1))
        full_out = whole_of(out_proj)
    spread = lax.dynamic_update_slice(
        jnp.zeros((dp_count * shard_rows, 128), jnp.bfloat16),
        extras,
        (lax.axis_index("dp") * shard_rows, 0),
    )
    extra_full = lax.psum(spread, "dp")
    codes = slot_codes(routes, drop_rank.reshape(tok_rows, top_count), expert_total, capacity)
    wide_codes = jnp.pad(codes, ((0, 0), (0, 128 - expert_total))).astype(jnp.bfloat16)
    q_width = query_proj.shape[1]
    extra_at = q_width + 2 * kv_width
    full_router = extra_full[:, :expert_total]
    gain_one = extra_full[:, expert_total]
    gain_two = extra_full[:, expert_total + 1]
    grad_all = lax.all_gather(grad_out, "expert", axis=0, tiled=True)
    gain_one = gain_one.astype(jnp.float32)
    gain_two = gain_two.astype(jnp.float32)
    inputs = layer_in.astype(jnp.float32)
    normed_full, inverse_one = norm_forward(inputs, gain_one)
    normed = normed_full.astype(jnp.bfloat16)
    row_index = jnp.arange(tok_rows, dtype=jnp.int32)
    parity = owner_index % 2
    position = jnp.where(
        row_index < prompt_rows,
        owner_index * prompt_rows + row_index,
        prompt_total + parity * half_rows + row_index - prompt_rows,
    )
    place = jnp.stack(
        [owner_index * prompt_rows, parity, owner_index * local_experts]
    ).astype(jnp.int32)
    cosines, sines = pair_tables(position)
    projected = project(normed, fused, cosines, sines)
    if small_plane:
        prompt_pairs, tail_pairs = share_pairs(projected)
    else:
        own_pairs = projected[:, q_width:]
        prompt_pairs = lax.all_gather(own_pairs[:prompt_rows], "expert", axis=0, tiled=True)
        ahead = [(source, source + 1) for source in range(0, owner_count, 2)]
        partner_pairs = lax.ppermute(own_pairs[prompt_rows:], "expert", ahead)
        tail_pairs = jnp.concatenate([partner_pairs, own_pairs[prompt_rows:]], axis=0)
    att_low, stats = attend(place, projected, prompt_pairs, tail_pairs)
    attn_proj = jnp.dot(att_low, full_out, preferred_element_type=jnp.float32)
    mixed_rows = inputs + RESIDUAL * attn_proj
    ffn_full, inverse_two = norm_forward(mixed_rows, gain_two)
    ffn_low = ffn_full.astype(jnp.bfloat16)

    def by_piece(values):
        turned = values.T.reshape(dp_count, owner_count, piece_rows, tok_rows)
        return turned.transpose(1, 0, 2, 3).reshape(width, tok_rows)

    normed_across, ffn_across, att_across = by_piece(normed), by_piece(ffn_low), by_piece(att_low)
    ffn_low, grad_all, normed_across, ffn_across, att_across = lax.optimization_barrier(
        (ffn_low, grad_all, normed_across, ffn_across, att_across)
    )
    gates = gates_of(
        jnp.dot(ffn_low, full_router, preferred_element_type=jnp.float32), codes
    )
    if owner_count == 8:
        input_rows, mixed_grad, acted_low, ffn_all = gathering_experts(
            jnp.concatenate([ffn_low, wide_codes], axis=1),
            grad_all,
            gate_up,
            down_proj,
            extra_full,
        )
    else:
        ffn_all = lax.all_gather(ffn_low, "expert", axis=0, tiled=True)
        codes_all = lax.all_gather(wide_codes, "expert", axis=0, tiled=True)
        input_rows, mixed_grad, acted_low = experts(
            place, ffn_all, grad_all, gate_up, down_proj, extra_full, codes_all
        )
    back_rows = lax.psum_scatter(
        input_rows, "expert", scatter_dimension=0, tiled=True
    ).astype(jnp.float32)
    over_tokens = (((0,), (0,)), ((), ()))

    def summed_over_tokens(left, right):
        return lax.dot_general(left, right, over_tokens, preferred_element_type=jnp.float32)

    gateup_low = [
        summed_over_tokens(ffn_all, mixed_grad[local]).astype(jnp.bfloat16)
        for local in range(local_experts)
    ]

    def down_part(act):
        return (RESIDUAL * summed_over_tokens(act, grad_all)).astype(jnp.bfloat16)

    down_first = down_part(acted_low[0])
    unit = width // 96
    parts = [
        (gateup_low[0][: 57 * unit],),
        (gateup_low[0][57 * unit :], gateup_low[1][: 25 * unit]),
        (gateup_low[1][25 * unit : 83 * unit],),
        (gateup_low[1][83 * unit :], down_first),
    ]

    def next_sum(part, sums):
        part, last = lax.optimization_barrier((part, sums[-1]))
        return [*sums[:-1], last, lax.psum(part, "dp")]

    sums = [lax.psum(parts[0], "dp")]
    back_rows, sums = lax.optimization_barrier((back_rows, sums))
    moe_part = moe_shares(acted_low, down_proj)
    sums = next_sum(parts[1], sums)
    upstream = grad_out.astype(jnp.float32)
    gate_grad = (
        back_rows[:, width : width + expert_total]
        + back_rows[:, width + 64 : width + 64 + expert_total]
    )
    logit_grad = (
        gates * (gate_grad - jnp.sum(gates * gate_grad, axis=1, keepdims=True))
    ).astype(jnp.bfloat16)
    ffn_grad = jnp.einsum("te,de->td", logit_grad, full_router, preferred_element_type=jnp.float32)
    ffn_grad = ffn_grad + back_rows[:, :width]
    norm_part, gain_two_local = norm_backward(mixed_rows, inverse_two, gain_two, ffn_grad)
    mixed_grad_total = upstream + norm_part
    attn_grad_low = (RESIDUAL * mixed_grad_total).astype(jnp.bfloat16)
    attended_grad = jnp.einsum(
        "td,cd->tc", attn_grad_low, full_out, preferred_element_type=jnp.float32
    ).astype(jnp.bfloat16)
    attended_grad, moe_part, parts = lax.optimization_barrier((attended_grad, moe_part, parts))
    moe_rows = lax.psum_scatter(moe_part, "expert", scatter_dimension=0, tiled=True)
    query_grad_low, prompt_key_part, prompt_value_part, tail_key_part, tail_value_part = (
        attend_back(
            place, projected, attended_grad, prompt_pairs, tail_pairs, stats, cosines, sines
        )
    )
    if small_plane:
        pair_grad_low = return_pairs(
            prompt_key_part, prompt_value_part, tail_key_part, tail_value_part, cosines, sines
        )
    else:
        prompt_grad = lax.psum_scatter(
            jnp.concatenate([prompt_key_part, prompt_value_part], axis=1),
            "expert",
            scatter_dimension=0,
            tiled=True,
        ).astype(jnp.float32)
        tail_part = jnp.concatenate([tail_key_part, tail_value_part], axis=1)
        behind = [(source + 1, source) for source in range(0, owner_count, 2)]
        tail_grad = tail_part[half_rows:] + lax.ppermute(
            tail_part[:half_rows].astype(jnp.bfloat16), "expert", behind
        ).astype(jnp.float32)
        pair_grad = jnp.concatenate([prompt_grad, tail_grad], axis=0)
        cosine, sine_part = rotary_tables(position, head_size)
        key_grad = unrotate(
            pair_grad[:, :kv_width].reshape(tok_rows, kv_heads, head_size), cosine, sine_part
        ).reshape(tok_rows, kv_width)
        pair_grad_low = jnp.concatenate(
            [key_grad, pair_grad[:, kv_width:]], axis=1
        ).astype(jnp.bfloat16)
    all_grad = jnp.concatenate(
        [
            query_grad_low,
            pair_grad_low,
            jnp.pad(logit_grad, ((0, 0), (0, 128 - expert_total))),
        ],
        axis=1,
    )
    normed_grad = jnp.einsum(
        "tc,dc->td",
        all_grad[:, :extra_at],
        fused,
        preferred_element_type=jnp.float32,
    )
    input_part, gain_one_local = norm_backward(inputs, inverse_one, gain_one, normed_grad)
    input_grad = (mixed_grad_total + input_part).astype(jnp.bfloat16)

    extra = jnp.stack([gain_one_local, gain_two_local], axis=1)
    extra = extra.reshape(dp_count, owner_count, piece_rows, 2).transpose(1, 0, 2, 3)
    extra = jnp.pad(
        extra.reshape(width, 2), ((0, 0), (expert_total, 126 - expert_total))
    )
    extra, moe_rows, sums = lax.optimization_barrier((extra, moe_rows, sums))
    sums = next_sum(parts[2], sums)
    layer_out = (mixed_rows + RESIDUAL * moe_rows.astype(jnp.float32)).astype(jnp.bfloat16)
    late_local = dense_weight_grads(
        normed_across, ffn_across, att_across, all_grad, attn_grad_low, extra
    )
    act_second, late_local = lax.optimization_barrier((acted_low[1], late_local))
    late = lax.psum_scatter(late_local, "expert", scatter_dimension=0, tiled=True)
    second_low = down_part(act_second)
    if small_plane:
        chunks = second_low.reshape(8, hidden_units // 8, width)
        second_sum = line_sum(dp_count, 6, chunks).reshape(hidden_units, width)
    else:
        second_sum = lax.psum(second_low, "dp").astype(jnp.float32)
    late, sums, second_sum = lax.optimization_barrier((late, sums, second_sum))
    sums = next_sum(parts[3], sums)
    if small_plane:
        late = line_scatter(late)
    else:
        late = lax.psum_scatter(late, "dp", scatter_dimension=0, tiled=True)
    late = lax.all_gather(late, "expert", axis=0, tiled=True).astype(jnp.float32)
    gateup_grad = jnp.stack(
        [
            jnp.concatenate([sums[0][0], sums[1][0]], axis=0),
            jnp.concatenate([sums[1][1], sums[2][0], sums[3][0]], axis=0),
        ]
    ).astype(jnp.float32)
    down_grad = jnp.stack([sums[3][1].astype(jnp.float32), second_sum])
    dense_grads = (
        late[:, extra_at + expert_total],
        late[:, :q_width],
        late[:, q_width : q_width + kv_width],
        late[:, q_width + kv_width : extra_at],
        late[:, extra_at + 128 :],
        late[:, extra_at + expert_total + 1],
        late[:, extra_at : extra_at + expert_total],
    )
    return (
        layer_out,
        input_grad,
        dense_grads[0],
        dense_grads[1],
        dense_grads[2],
        dense_grads[3],
        dense_grads[4],
        dense_grads[5],
        dense_grads[6],
        gateup_grad,
        down_grad,
    )


def solution(mesh):
    placed = (
        P(("dp", "expert"), None),
        P(("dp", "expert"), None),
        P("dp"),
        P("dp", None),
        P("dp", None),
        P("dp", None),
        P("dp", None),
        P("dp"),
        P("dp", None),
        P("expert", None, None),
        P("expert", None, None),
        P(("dp", "expert"), None),
        P(("dp", "expert"), None),
    )
    return jax.shard_map(
        on_device,
        mesh=mesh,
        in_specs=placed,
        out_specs=(
            P(("dp", "expert"), None),
            P(("dp", "expert"), None),
            P("dp"),
            P("dp", None),
            P("dp", None),
            P("dp", None),
            P("dp", None),
            P("dp"),
            P("dp", None),
            P("expert", None, None),
            P("expert", None, None),
        ),
        check_vma=False,
    )
```
